32 devices in a mesh: row: 2 (over y), col: 16 (over z, x, core).
Axes of the slice: x: 2, y: 2, z: 4, core: 2. Of those that a mesh axis runs over, the one named last changes fastest.
Arguments:
- queries: bfloat16 [8192, 1024], P(('row', 'col')), may hold values from -8 to 8
- key_rows: bfloat16 [8192, 1024], P(('row', 'col')), may hold values from -8 to 8
- value_rows: bfloat16 [8192, 1024], P(('row', 'col')), may hold values from -6 to 6
- out_grad: bfloat16 [8192, 1024], P(('row', 'col')), may hold values from -6 to 6
- dropout_bits: int32 [8192, 128], P(('row', 'col')), may hold values from 0 to 255, as said below
- partner: int32 [3, 2, 16], replicated, may hold values from 0 to 15, each once within a row
- block_pick: int32 [3, 2, 16], replicated, may hold values from 0 to 1
- global_blocks: int32 [2], replicated, may hold values from 0 to 63
Outputs:
- attended: bfloat16 [8192, 1024], P(('row', 'col'))
- query_grad: bfloat16 [8192, 1024], P(('row', 'col'))
- key_grad: bfloat16 [8192, 1024], P(('row', 'col'))
- value_grad: bfloat16 [8192, 1024], P(('row', 'col'))
The draws below stay inside these ranges and needn't reach their ends.
Inputs may be any that keep to these rules, and one draw needn't show every extreme that they name: `dropout_bits`: each word packs 8 flags of 0 or 1 in its low bits. partner[r, a, :] is a permutation of the places 0 to 15.
All inputs are finite; a program needn't handle non-finite values.
Results may differ from the reference program's by a relative error of at most 0.0085.
Values may be sent and summed in bfloat16 or wider, within the bound.
A program may use at most 128 MiB of HBM per device.

```python
import jax
import jax.numpy as jnp
from jax import lax

HEADS = 16
HEAD_DIM = 64
BLOCK = 128
NGLOBAL = 2
NMATCH = 3
TOK_DEV = 256
WIDTH = 1024
BANDS = 2
PEERS = 16
TOKENS = 8192
NBLOCKS = 64
BLK_DEV = 2
SLOTS = 8
WORDS = 128


def draw_queries(key, part):
    base = jnp.clip(jax.random.normal(jax.random.fold_in(key, 1), (TOKENS, WIDTH), jnp.float32), -4.0, 4.0)
    return base.astype(jnp.bfloat16)


def draw_key_rows(key, part):
    base = jnp.clip(jax.random.normal(jax.random.fold_in(key, 2), (TOKENS, WIDTH), jnp.float32), -4.0, 4.0)
    return base.astype(jnp.bfloat16)


def draw_dropout_bits(key, part):
    rolls = jax.random.randint(jax.random.fold_in(key, 3), (TOKENS, WORDS, 8), 0, 10)
    kept = (rolls != 0).astype(jnp.int32)
    weights = jnp.left_shift(jnp.ones((8,), jnp.int32), jnp.arange(8, dtype=jnp.int32))
    return jnp.sum(kept * weights, -1).astype(jnp.int32)


def place_ends(values, stream_key, low, top_value):
    shape = values.shape
    index_at = [jax.random.randint(jax.random.fold_in(stream_key, axis), (), 0, shape[axis]) for axis in range(len(shape))]
    values = values.at[tuple(index_at)].set(low)
    longest = shape.index(max(shape))
    index_at[longest] = (index_at[longest] + 1) % shape[longest]
    return values.at[tuple(index_at)].set(top_value)


def block_scale(stream_key, dims, pieces, least, largest):
    gain, own = 1.0, jax.random.fold_in(stream_key, 6)
    for dim, shards_of in pieces:
        steps = jnp.exp(jax.random.uniform(jax.random.fold_in(own, dim), (shards_of,), jnp.float32, least / len(pieces), largest / len(pieces)))
        gain = gain * jnp.repeat(steps, dims[dim] // shards_of).reshape([-1 if axis == dim else 1 for axis in range(len(dims))])
    return gain


def gaussian(stream_key, dims, deviation, reach, pieces=(), kind=jnp.bfloat16):
    array = deviation * jax.random.normal(stream_key, dims, jnp.float32)
    if pieces:
        array = array * block_scale(stream_key, dims, pieces, -0.22, 0.18)
    return jnp.clip(array, -reach, reach).astype(kind)


def setup_inputs(seed: int = 0) -> dict:
    key_of = jax.random.split(jax.random.key(seed), 9)
    return {
        "queries": draw_queries(jax.random.fold_in(key_of[8], 71), 0),
        "key_rows": draw_key_rows(jax.random.fold_in(key_of[8], 71), 0),
        "value_rows": gaussian(key_of[2], (TOKENS, WIDTH), 1.0, 6.0, ((0, 32),)),
        "out_grad": gaussian(key_of[3], (TOKENS, WIDTH), 1.0, 6.0, ((0, 32),)),
        "dropout_bits": draw_dropout_bits(jax.random.fold_in(key_of[8], 71), 0),
        "partner": jax.vmap(lambda own: jax.random.permutation(own, PEERS))(jax.random.split(key_of[5], NMATCH * BANDS)).reshape((NMATCH, BANDS, PEERS)).astype(jnp.int32),
        "block_pick": place_ends(jax.random.randint(key_of[6], (NMATCH, BANDS, PEERS), 0, BLK_DEV), jax.random.fold_in(key_of[6], 1), 0, BLK_DEV - 1).astype(jnp.int32),
        "global_blocks": jax.random.randint(key_of[7], (NGLOBAL,), 0, NBLOCKS).astype(jnp.int32),
    }


score_scale = 0.125
keep_scale = 1.0 / 0.9


def unpack_bits(packed):
    shifts = jnp.arange(8, dtype=jnp.int32)
    flags = jnp.right_shift(packed[..., None], shifts) & 1
    return flags.reshape(packed.shape[:-1] + (packed.shape[-1] * 8,))


def round_trip(values):
    return lax.optimization_barrier(values.astype(jnp.bfloat16)).astype(jnp.float32)


def reference(queries, key_rows, value_rows, out_grad, dropout_bits, partner, block_pick, global_blocks):
    width_all = HEADS * HEAD_DIM
    both_rows = jnp.concatenate([key_rows, value_rows], 1).reshape(NBLOCKS, BLOCK, 2 * width_all)

    def segment_step(totals, segment):
        band_index = segment // PEERS
        place_index = segment % PEERS
        first = (segment * BLK_DEV).astype(jnp.int32)
        own_blocks = first + jnp.arange(BLK_DEV, dtype=jnp.int32)
        window_ids = jnp.stack([(own_blocks - 1) % NBLOCKS, own_blocks, (own_blocks + 1) % NBLOCKS], 1)
        random_ids = (band_index * PEERS + partner[:, band_index, place_index]) * BLK_DEV + block_pick[:, band_index, place_index]
        shared_ids = jnp.concatenate([global_blocks, random_ids]).astype(jnp.int32)
        slot_ids = jnp.concatenate([window_ids, jnp.broadcast_to(shared_ids[None, :], (BLK_DEV, NGLOBAL + NMATCH))], 1).astype(jnp.int32)
        gathered = both_rows[slot_ids].astype(jnp.float32).reshape(BLK_DEV, SLOTS * BLOCK, 2 * width_all)
        keys_f = gathered[..., :width_all].reshape(BLK_DEV, SLOTS * BLOCK, HEADS, HEAD_DIM)
        values_f = gathered[..., width_all:].reshape(BLK_DEV, SLOTS * BLOCK, HEADS, HEAD_DIM)
        start_row = (first * BLOCK).astype(jnp.int32)
        query_f = lax.dynamic_slice_in_dim(queries, start_row, TOK_DEV, 0).astype(jnp.float32).reshape(BLK_DEV, BLOCK, HEADS, HEAD_DIM)
        grad_f = lax.dynamic_slice_in_dim(out_grad, start_row, TOK_DEV, 0).astype(jnp.float32).reshape(BLK_DEV, BLOCK, HEADS, HEAD_DIM)
        words = lax.dynamic_slice_in_dim(dropout_bits, start_row, TOK_DEV, 0)
        keep_mask = (unpack_bits(words).astype(jnp.float32) * keep_scale).reshape(BLK_DEV, BLOCK, SLOTS * BLOCK)
        score = jnp.einsum('jqhd,jkhd->jhqk', query_f, keys_f) * score_scale
        top = jnp.max(score, -1, keepdims=True)
        log_total = top + jnp.log(jnp.sum(jnp.exp(score - top), -1, keepdims=True))
        probs = jnp.exp(score - log_total)
        dropped_f = round_trip(probs * keep_mask[:, None])
        attended = jnp.einsum('jhqk,jkhd->jqhd', dropped_f, values_f).astype(jnp.bfloat16).reshape(TOK_DEV, width_all)
        grad_p = jnp.einsum('jqhd,jkhd->jhqk', grad_f, values_f) * keep_mask[:, None]
        delta = jnp.sum(probs * grad_p, -1, keepdims=True)
        dscore = round_trip(probs * (grad_p - delta))
        query_grad = (score_scale * jnp.einsum('jhqk,jkhd->jqhd', dscore, keys_f)).astype(jnp.bfloat16).reshape(TOK_DEV, width_all)
        key_part = (score_scale * jnp.einsum('jhqk,jqhd->jkhd', dscore, query_f)).reshape(BLK_DEV, SLOTS, BLOCK, width_all)
        value_part = jnp.einsum('jhqk,jqhd->jkhd', dropped_f, grad_f).reshape(BLK_DEV, SLOTS, BLOCK, width_all)
        parts = jnp.concatenate([key_part, value_part], -1)
        nearby = jnp.zeros((BLK_DEV + 2, BLOCK, 2 * width_all), jnp.float32)
        for offset_slot in range(3):
            nearby = nearby.at[offset_slot:offset_slot + BLK_DEV].add(parts[:, offset_slot])
        totals = totals.at[own_blocks].add(nearby[1:BLK_DEV + 1])
        totals = totals.at[(first - 1) % NBLOCKS].add(round_trip(nearby[0]))
        totals = totals.at[(first + BLK_DEV) % NBLOCKS].add(round_trip(nearby[BLK_DEV + 1]))
        distant = jnp.sum(parts[:, 3:], 0)
        for global_slot in range(NGLOBAL):
            totals = totals.at[global_blocks[global_slot]].add(distant[global_slot])
        for matching in range(NMATCH):
            totals = totals.at[random_ids[matching]].add(round_trip(distant[NGLOBAL + matching]))
        return totals, (attended, query_grad)

    start_totals = jnp.zeros((NBLOCKS, BLOCK, 2 * width_all), jnp.float32)
    totals, (attended, query_grad) = lax.scan(segment_step, start_totals, jnp.arange(BANDS * PEERS, dtype=jnp.int32))
    totals = totals.reshape(TOKENS, 2 * width_all)
    return (attended.reshape(TOKENS, width_all), query_grad.reshape(TOKENS, width_all),
            totals[:, :width_all].astype(jnp.bfloat16), totals[:, width_all:].astype(jnp.bfloat16))
```

```python
import functools

import jax
import jax.numpy as jnp
from jax import lax
from jax.experimental import pallas as pl
from jax.experimental.pallas import tpu as pltpu
from jax.sharding import PartitionSpec as P

HEADS = 16
HEAD_DIM = 64
BLOCK = 128
NGLOBAL = 2
NMATCH = 3
PAIR = 2 * HEAD_DIM
SLOTS = 3 + NGLOBAL + NMATCH
CHUNKS = 1

score_scale = 0.125
keep_scale = 1.0 / 0.9


def contract(a, b, dim_a, dim_b):
    return lax.dot_general(a, b, (((dim_a,), (dim_b,)), ((), ())), preferred_element_type=jnp.float32)


def attention_kernel(
    blocks, q_ref, g_ref, ko_ref, vo_ref, kp_ref, vp_ref, kn_ref, vn_ref, kg_ref, vg_ref, kr_ref, vr_ref, bits_ref,
    att_ref, qg_ref, own_ref, rims_ref, far_ref,
    keep_ref, kall_ref, vall_ref, qall_ref, gall_ref, s_ref, dp_ref, p_ref, ds_ref,
):
    near = blocks + 2
    own_rows = blocks * BLOCK

    @pl.when(pl.program_id(0) == 0)
    def _():
        shifts = lax.broadcasted_iota(jnp.int32, (BLOCK // 8, 8, BLOCK), 1)
        for j in range(blocks):
            for i in range(SLOTS):
                words = bits_ref[j, i * BLOCK // 8 : (i + 1) * BLOCK // 8, :]
                flags = jnp.right_shift(jnp.broadcast_to(words[:, None, :], shifts.shape), shifts) & 1
                keep_ref[j, i] = (flags.astype(jnp.float32) * keep_scale).reshape(BLOCK, BLOCK)
        p_ref[...] = jnp.zeros_like(p_ref)
        ds_ref[...] = jnp.zeros_like(ds_ref)

    for all_ref, parts in ((kall_ref, (kp_ref, ko_ref, kn_ref, kg_ref, kr_ref)), (vall_ref, (vp_ref, vo_ref, vn_ref, vg_ref, vr_ref))):
        row = 0
        for part in parts:
            all_ref[row : row + part.shape[0], :] = part[...]
            row += part.shape[0]
    first = lax.broadcasted_iota(jnp.int32, (BLOCK, PAIR), 1) < HEAD_DIM
    zero = jnp.zeros((BLOCK, PAIR), jnp.bfloat16)
    for j in range(blocks):
        rows = slice(j * BLOCK, (j + 1) * BLOCK)
        query = (q_ref[rows, :].astype(jnp.float32) * score_scale).astype(jnp.bfloat16)
        grad = g_ref[rows, :]
        base = 2 * j * BLOCK
        qall_ref[base : base + BLOCK, :] = jnp.where(first, query, zero)
        qall_ref[base + BLOCK : base + 2 * BLOCK, :] = jnp.where(first, zero, query)
        gall_ref[base : base + BLOCK, :] = jnp.where(first, grad, zero)
        gall_ref[base + BLOCK : base + 2 * BLOCK, :] = jnp.where(first, zero, grad)

    wide = 2 * BLOCK
    for j in range(blocks):
        cols = slice(j * wide, (j + 1) * wide)
        places = [j, j + 1, j + 2] + list(range(near, near + NGLOBAL + NMATCH))
        query = qall_ref[cols, :]
        grad = gall_ref[cols, :]
        top = None
        for i, b in enumerate(places):
            score = contract(kall_ref[b * BLOCK : (b + 1) * BLOCK, :], query, 1, 1)
            s_ref[i] = score
            part = jnp.max(score.reshape(BLOCK // 8, 8, wide), axis=0)
            top = part if top is None else jnp.maximum(top, part)
        top = jnp.max(top, axis=0, keepdims=True)
        total, mixed = None, None
        for i, b in enumerate(places):
            keep = keep_ref[j, i]
            keep = jnp.concatenate([keep, keep], axis=1)
            weight = jnp.exp(s_ref[i] - top)
            s_ref[i] = weight
            grad_p = contract(vall_ref[b * BLOCK : (b + 1) * BLOCK, :], grad, 1, 1) * keep
            dp_ref[i] = grad_p
            part = jnp.sum(weight.reshape(BLOCK // 8, 8, wide), axis=0)
            cross = jnp.sum((weight * grad_p).reshape(BLOCK // 8, 8, wide), axis=0)
            total = part if total is None else total + part
            mixed = cross if mixed is None else mixed + cross
        inverse = 1.0 / jnp.sum(total, axis=0, keepdims=True)
        delta = jnp.sum(mixed, axis=0, keepdims=True) * inverse
        for i, b in enumerate(places):
            keep = keep_ref[j, i]
            keep = jnp.concatenate([keep, keep], axis=1)
            probs = s_ref[i] * inverse
            p_ref[b * BLOCK : (b + 1) * BLOCK, cols] = (probs * keep).astype(jnp.bfloat16)
            ds_ref[b * BLOCK : (b + 1) * BLOCK, cols] = (probs * (dp_ref[i] - delta)).astype(jnp.bfloat16)

    out_t = contract(vall_ref[...], p_ref[...], 0, 0)
    qg_t = contract(kall_ref[...], ds_ref[...], 0, 0) * score_scale
    for j in range(blocks):
        rows = slice(j * BLOCK, (j + 1) * BLOCK)
        base = j * wide
        for result, ref in ((out_t, att_ref), (qg_t, qg_ref)):
            picked = jnp.concatenate(
                [result[:HEAD_DIM, base : base + BLOCK], result[HEAD_DIM:, base + BLOCK : base + wide]], axis=0
            )
            ref[rows, :] = picked.T.astype(jnp.bfloat16)
    for which, (left, right) in enumerate(((ds_ref, qall_ref), (p_ref, gall_ref))):
        grads = contract(left[...], right[...], 1, 0)
        own_ref[which] = grads[BLOCK : BLOCK + own_rows]
        rims_ref[which, :BLOCK] = grads[:BLOCK].astype(jnp.bfloat16)
        rims_ref[which, BLOCK:] = grads[BLOCK + own_rows : near * BLOCK].astype(jnp.bfloat16)
        far_ref[which] = grads[near * BLOCK :].astype(jnp.bfloat16)


def attention(queries, out_grad, key_rows, value_rows, before, after, shared, fetched, bits, chunk):
    tokens_here, width = queries.shape
    blocks = tokens_here // BLOCK
    pairs = width // PAIR // CHUNKS
    start = chunk * pairs
    part_width = width // CHUNKS
    far_rows = (NGLOBAL + NMATCH) * BLOCK
    all_rows = (blocks + 2) * BLOCK + far_rows

    def plain(rows):
        return pl.BlockSpec((rows, PAIR), lambda h: (0, start + h))

    def halves(rows):
        return [pl.BlockSpec((rows, PAIR), lambda h: (0, h)), pl.BlockSpec((rows, PAIR), lambda h: (0, pairs + h))]

    def out(rows, kind):
        return pl.BlockSpec((2, rows, PAIR), lambda h: (0, 0, h)), jax.ShapeDtypeStruct((2, rows, part_width), kind)

    flat = pl.BlockSpec((tokens_here, PAIR), lambda h: (0, h)), jax.ShapeDtypeStruct((tokens_here, part_width), jnp.bfloat16)
    outs = [flat, flat, out(tokens_here, jnp.float32), out(2 * BLOCK, jnp.bfloat16), out(far_rows, jnp.bfloat16)]
    pair_work = HEADS // CHUNKS * tokens_here * SLOTS * BLOCK
    return pl.pallas_call(
        functools.partial(attention_kernel, blocks),
        grid=(pairs,),
        in_specs=[plain(tokens_here)] * 4
        + halves(BLOCK) + halves(BLOCK) + halves(NGLOBAL * BLOCK) + halves(NMATCH * BLOCK)
        + [pl.BlockSpec(bits.shape, lambda h: (0, 0, 0))],
        out_specs=[spec for spec, _ in outs],
        out_shape=[shape for _, shape in outs],
        scratch_shapes=[
            pltpu.VMEM((blocks, SLOTS, BLOCK, BLOCK), jnp.float32),
            pltpu.VMEM((all_rows, PAIR), jnp.bfloat16),
            pltpu.VMEM((all_rows, PAIR), jnp.bfloat16),
            pltpu.VMEM((2 * tokens_here, PAIR), jnp.bfloat16),
            pltpu.VMEM((2 * tokens_here, PAIR), jnp.bfloat16),
            pltpu.VMEM((SLOTS, BLOCK, 2 * BLOCK), jnp.float32),
            pltpu.VMEM((SLOTS, BLOCK, 2 * BLOCK), jnp.float32),
            pltpu.VMEM((all_rows, 2 * tokens_here), jnp.bfloat16),
            pltpu.VMEM((all_rows, 2 * tokens_here), jnp.bfloat16),
        ],
        cost_estimate=pl.CostEstimate(
            flops=pair_work * HEAD_DIM * 2 * 7, bytes_accessed=16 * tokens_here * part_width, transcendentals=pair_work
        ),
        name="block_attention",
    )(queries, out_grad, key_rows, value_rows, before, before, after, after, shared, shared, fetched, fetched, bits)


def exchange(pieces):
    return lax.all_to_all(pieces, "col", split_axis=0, concat_axis=0, tiled=True)


def body(queries, key_rows, value_rows, out_grad, dropout_bits, partner, block_pick, global_blocks):
    tokens_here, width = queries.shape
    blocks = tokens_here // BLOCK
    bands, cols = lax.axis_size("row"), lax.axis_size("col")
    band, place = lax.axis_index("row"), lax.axis_index("col")
    rows = BLOCK // cols
    part = width // CHUNKS
    size = bands * cols
    up = [(i, (i + 1) % size) for i in range(size)]
    down = [(j, i) for i, j in up]
    ordering = lax.dynamic_index_in_dim(partner, band, 1, keepdims=False)
    picks = lax.dynamic_index_in_dim(block_pick, band, 1, keepdims=False)
    col_ids = jnp.arange(cols, dtype=jnp.int32)
    hits = ordering[:, :, None] == col_ids[None, None, :]
    inverse = jnp.sum(jnp.where(hits, col_ids[None, :, None], 0), axis=1)
    asked = jnp.sum(jnp.where(hits, picks[:, :, None], 0), axis=1)
    wanted_ids = (ordering * blocks + picks).T.reshape(-1)
    band_start = band * cols * blocks
    global_ids = jnp.clip(global_blocks - band_start, 0, cols * blocks - 1)
    bits = dropout_bits.reshape(blocks, BLOCK, -1).swapaxes(1, 2)
    attended, query_grad, key_grad, value_grad = [], [], [], []
    for chunk in range(CHUNKS):
        lower, upper = chunk * part, (chunk + 1) * part
        both = jnp.concatenate([key_rows[:, lower:upper], value_rows[:, lower:upper]], 1)
        spread = exchange(both.reshape(blocks, cols, rows, 2 * part).swapaxes(0, 1))
        strips = spread.reshape(cols * blocks, rows, 2 * part)
        global_strips = jnp.take(strips, global_ids, axis=0)
        gathered = lax.all_gather(global_strips, ("row", "col"), axis=0, tiled=False)
        gathered = gathered.reshape(bands, cols, NGLOBAL, rows, 2 * part)
        shared = jnp.concatenate(
            [
                lax.dynamic_index_in_dim(
                    gathered[:, :, g], global_blocks[g] // (cols * blocks), 0, keepdims=False
                ).reshape(BLOCK, 2 * part)
                for g in range(NGLOBAL)
            ],
            0,
        )
        sent = jnp.take(strips, wanted_ids, axis=0).reshape(cols, NMATCH, rows, 2 * part)
        fetched = exchange(sent).swapaxes(0, 1).reshape(NMATCH * BLOCK, 2 * part)
        before = lax.ppermute(both[tokens_here - BLOCK :], ("row", "col"), up)
        after = lax.ppermute(both[:BLOCK], ("row", "col"), down)
        att, qgrad, own, rims, far = attention(
            queries, out_grad, key_rows, value_rows, before, after, shared, fetched, bits, chunk
        )
        attended.append(att)
        query_grad.append(qgrad)
        from_next = lax.ppermute(rims[:, :BLOCK], ("row", "col"), down)
        from_last = lax.ppermute(rims[:, BLOCK:], ("row", "col"), up)
        slots = NGLOBAL + NMATCH
        pieces = far.reshape(2, slots, cols, rows, part).transpose(2, 1, 0, 3, 4)
        landed = exchange(pieces)
        band_sum = jnp.sum(landed[:, :NGLOBAL].astype(jnp.float32), axis=0)
        global_sum = band_sum
        for step in range(1, bands):
            ring = [(i, (i + step) % bands) for i in range(bands)]
            global_sum = global_sum + lax.ppermute(band_sum, "row", ring)
        block_ids = (band_start + jnp.arange(cols * blocks, dtype=jnp.int32)).reshape(cols, blocks)
        local_ids = jnp.arange(blocks, dtype=jnp.int32)
        returned = jnp.zeros((cols, blocks, 2, rows, part), jnp.float32)
        for matching in range(NMATCH):
            moved = jnp.take(landed[:, NGLOBAL + matching], inverse[matching], axis=0).astype(jnp.float32)
            mine = asked[matching][:, None] == local_ids[None, :]
            returned = returned + jnp.where(mine[:, :, None, None, None], moved[:, None], 0.0)
        for g in range(NGLOBAL):
            mine = block_ids == global_blocks[g]
            returned = returned + jnp.where(mine[:, :, None, None, None], global_sum[g][None, None], 0.0)
        home = exchange(returned.astype(jnp.bfloat16)).transpose(2, 1, 0, 3, 4).reshape(2, tokens_here, part)
        total = own + home.astype(jnp.float32)
        room = ((0, 0), (0, tokens_here - BLOCK), (0, 0))
        total = total + jnp.pad(from_last.astype(jnp.float32), room)
        total = total + jnp.pad(from_next.astype(jnp.float32), (room[0], room[1][::-1], room[2]))
        key_grad.append(total[0].astype(jnp.bfloat16))
        value_grad.append(total[1].astype(jnp.bfloat16))
    return tuple(jnp.concatenate(parts, 1) for parts in (attended, query_grad, key_grad, value_grad))


def solution(mesh):
    split = P(("row", "col"), None)
    return jax.shard_map(
        body,
        mesh=mesh,
        in_specs=(split,) * 5 + (P(),) * 3,
        out_specs=(split,) * 4,
        check_vma=False,
    )
```

```python
import functools

import jax
import jax.numpy as jnp
from jax import lax
from jax.experimental import pallas as pl
from jax.experimental.pallas import tpu as pltpu
from jax.sharding import PartitionSpec as P

HEADS = 16
HEAD_DIM = 64
BLOCK = 128
NGLOBAL = 2
NMATCH = 3
PAIR = 2 * HEAD_DIM
SLOTS = 3 + NGLOBAL + NMATCH
CHUNKS = 1

score_scale = 0.125
keep_scale = 1.0 / 0.9


def contract(a, b, dim_a, dim_b):
    return lax.dot_general(a, b, (((dim_a,), (dim_b,)), ((), ())), preferred_element_type=jnp.float32)


def attention_kernel(
    blocks, q_ref, g_ref, ko_ref, vo_ref, kp_ref, vp_ref, kn_ref, vn_ref, kg_ref, vg_ref, kr_ref, vr_ref, bits_ref,
    att_ref, qg_ref, own_ref, rims_ref, far_ref,
    keep_ref, kall_ref, vall_ref, qall_ref, gall_ref, s_ref, dp_ref, p_ref, ds_ref,
):
    near = blocks + 2
    own_rows = blocks * BLOCK

    @pl.when(pl.program_id(0) == 0)
    def _():
        shifts = lax.broadcasted_iota(jnp.int32, (BLOCK // 8, 8, BLOCK), 1)
        for j in range(blocks):
            for i in range(SLOTS):
                words = bits_ref[j, i * BLOCK // 8 : (i + 1) * BLOCK // 8, :]
                flags = jnp.right_shift(jnp.broadcast_to(words[:, None, :], shifts.shape), shifts) & 1
                keep_ref[j, i] = (flags.astype(jnp.float32) * keep_scale).reshape(BLOCK, BLOCK)
        p_ref[...] = jnp.zeros_like(p_ref)
        ds_ref[...] = jnp.zeros_like(ds_ref)

    for all_ref, parts in ((kall_ref, (kp_ref, ko_ref, kn_ref, kg_ref, kr_ref)), (vall_ref, (vp_ref, vo_ref, vn_ref, vg_ref, vr_ref))):
        row = 0
        for part in parts:
            all_ref[row : row + part.shape[0], :] = part[...]
            row += part.shape[0]
    first = lax.broadcasted_iota(jnp.int32, (BLOCK, PAIR), 1) < HEAD_DIM
    zero = jnp.zeros((BLOCK, PAIR), jnp.bfloat16)
    for j in range(blocks):
        rows = slice(j * BLOCK, (j + 1) * BLOCK)
        query = (q_ref[rows, :].astype(jnp.float32) * score_scale).astype(jnp.bfloat16)
        grad = g_ref[rows, :]
        base = 2 * j * BLOCK
        qall_ref[base : base + BLOCK, :] = jnp.where(first, query, zero)
        qall_ref[base + BLOCK : base + 2 * BLOCK, :] = jnp.where(first, zero, query)
        gall_ref[base : base + BLOCK, :] = jnp.where(first, grad, zero)
        gall_ref[base + BLOCK : base + 2 * BLOCK, :] = jnp.where(first, zero, grad)

    wide = 2 * BLOCK
    for j in range(blocks):
        cols = slice(j * wide, (j + 1) * wide)
        places = [j, j + 1, j + 2] + list(range(near, near + NGLOBAL + NMATCH))
        query = qall_ref[cols, :]
        grad = gall_ref[cols, :]
        top = None
        for i, b in enumerate(places):
            score = contract(kall_ref[b * BLOCK : (b + 1) * BLOCK, :], query, 1, 1)
            s_ref[i] = score
            part = jnp.max(score.reshape(BLOCK // 8, 8, wide), axis=0)
            top = part if top is None else jnp.maximum(top, part)
        top = jnp.max(top, axis=0, keepdims=True)
        total, mixed = None, None
        for i, b in enumerate(places):
            keep = keep_ref[j, i]
            keep = jnp.concatenate([keep, keep], axis=1)
            weight = jnp.exp(s_ref[i] - top)
            s_ref[i] = weight
            grad_p = contract(vall_ref[b * BLOCK : (b + 1) * BLOCK, :], grad, 1, 1) * keep
            dp_ref[i] = grad_p
            part = jnp.sum(weight.reshape(BLOCK // 8, 8, wide), axis=0)
            cross = jnp.sum((weight * grad_p).reshape(BLOCK // 8, 8, wide), axis=0)
            total = part if total is None else total + part
            mixed = cross if mixed is None else mixed + cross
        inverse = 1.0 / jnp.sum(total, axis=0, keepdims=True)
        delta = jnp.sum(mixed, axis=0, keepdims=True) * inverse
        for i, b in enumerate(places):
            keep = keep_ref[j, i]
            keep = jnp.concatenate([keep, keep], axis=1)
            probs = s_ref[i] * inverse
            p_ref[b * BLOCK : (b + 1) * BLOCK, cols] = (probs * keep).astype(jnp.bfloat16)
            ds_ref[b * BLOCK : (b + 1) * BLOCK, cols] = (probs * (dp_ref[i] - delta)).astype(jnp.bfloat16)

    out_t = contract(vall_ref[...], p_ref[...], 0, 0)
    qg_t = contract(kall_ref[...], ds_ref[...], 0, 0) * score_scale
    for j in range(blocks):
        rows = slice(j * BLOCK, (j + 1) * BLOCK)
        base = j * wide
        for result, ref in ((out_t, att_ref), (qg_t, qg_ref)):
            picked = jnp.concatenate(
                [result[:HEAD_DIM, base : base + BLOCK], result[HEAD_DIM:, base + BLOCK : base + wide]], axis=0
            )
            ref[rows, :] = picked.T.astype(jnp.bfloat16)
    for which, (left, right) in enumerate(((ds_ref, qall_ref), (p_ref, gall_ref))):
        grads = contract(left[...], right[...], 1, 0)
        own_ref[which] = grads[BLOCK : BLOCK + own_rows]
        rims_ref[which, :BLOCK] = grads[:BLOCK].astype(jnp.bfloat16)
        rims_ref[which, BLOCK:] = grads[BLOCK + own_rows : near * BLOCK].astype(jnp.bfloat16)
        far_ref[which] = grads[near * BLOCK :].astype(jnp.bfloat16)


def attention(queries, out_grad, key_rows, value_rows, before, after, shared, fetched, bits, chunk):
    tokens_here, width = queries.shape
    blocks = tokens_here // BLOCK
    pairs = width // PAIR // CHUNKS
    start = chunk * pairs
    part_width = width // CHUNKS
    far_rows = (NGLOBAL + NMATCH) * BLOCK
    all_rows = (blocks + 2) * BLOCK + far_rows

    def plain(rows):
        return pl.BlockSpec((rows, PAIR), lambda h: (0, start + h))

    def halves(rows):
        return [pl.BlockSpec((rows, PAIR), lambda h: (0, h)), pl.BlockSpec((rows, PAIR), lambda h: (0, pairs + h))]

    def out(rows, kind):
        return pl.BlockSpec((2, rows, PAIR), lambda h: (0, 0, h)), jax.ShapeDtypeStruct((2, rows, part_width), kind)

    flat = pl.BlockSpec((tokens_here, PAIR), lambda h: (0, h)), jax.ShapeDtypeStruct((tokens_here, part_width), jnp.bfloat16)
    outs = [flat, flat, out(tokens_here, jnp.float32), out(2 * BLOCK, jnp.bfloat16), out(far_rows, jnp.bfloat16)]
    pair_work = HEADS // CHUNKS * tokens_here * SLOTS * BLOCK
    return pl.pallas_call(
        functools.partial(attention_kernel, blocks),
        grid=(pairs,),
        in_specs=[plain(tokens_here)] * 4
        + halves(BLOCK) + halves(BLOCK) + halves(NGLOBAL * BLOCK) + halves(NMATCH * BLOCK)
        + [pl.BlockSpec(bits.shape, lambda h: (0, 0, 0))],
        out_specs=[spec for spec, _ in outs],
        out_shape=[shape for _, shape in outs],
        scratch_shapes=[
            pltpu.VMEM((blocks, SLOTS, BLOCK, BLOCK), jnp.float32),
            pltpu.VMEM((all_rows, PAIR), jnp.bfloat16),
            pltpu.VMEM((all_rows, PAIR), jnp.bfloat16),
            pltpu.VMEM((2 * tokens_here, PAIR), jnp.bfloat16),
            pltpu.VMEM((2 * tokens_here, PAIR), jnp.bfloat16),
            pltpu.VMEM((SLOTS, BLOCK, 2 * BLOCK), jnp.float32),
            pltpu.VMEM((SLOTS, BLOCK, 2 * BLOCK), jnp.float32),
            pltpu.VMEM((all_rows, 2 * tokens_here), jnp.bfloat16),
            pltpu.VMEM((all_rows, 2 * tokens_here), jnp.bfloat16),
        ],
        cost_estimate=pl.CostEstimate(
            flops=pair_work * HEAD_DIM * 2 * 7, bytes_accessed=16 * tokens_here * part_width, transcendentals=pair_work
        ),
        name="block_attention",
    )(queries, out_grad, key_rows, value_rows, before, before, after, after, shared, shared, fetched, fetched, bits)


def partner_of(me, bit):
    flag = (me // 2**bit) % 2
    return flag, me + 2**bit - 2 * 2**bit * flag


def greet(me, levels):
    barrier = pltpu.get_barrier_semaphore()
    for bit in range(levels):
        pl.semaphore_signal(barrier, inc=1, device_id={"col": partner_of(me, bit)[1]})
    pl.semaphore_wait(barrier, levels)


def gather_kernel(levels, strip_ref, all_ref, send_sem, recv_sem):
    me = lax.axis_index("col")
    greet(me, levels)
    flags = [partner_of(me, levels - 1 - d)[0] for d in range(levels)]
    pick = pl.ds
    here = tuple(pick(flag, 1) for flag in flags)
    all_ref[here] = strip_ref[...].reshape((1,) * levels + strip_ref.shape)
    for dim in range(levels):
        region = (slice(None),) * dim + here[dim:]
        copy = pltpu.make_async_remote_copy(
            src_ref=all_ref.at[region],
            dst_ref=all_ref.at[region],
            send_sem=send_sem.at[dim],
            recv_sem=recv_sem.at[dim],
            device_id={"col": partner_of(me, levels - 1 - dim)[1]},
        )
        copy.start()
        copy.wait()


def gather_strips(strip, cols):
    levels = cols.bit_length() - 1
    vmem = pl.BlockSpec(memory_space=pltpu.VMEM)
    out = pl.pallas_call(
        functools.partial(gather_kernel, levels),
        out_shape=jax.ShapeDtypeStruct((2,) * levels + strip.shape, strip.dtype),
        in_specs=[vmem],
        out_specs=vmem,
        scratch_shapes=[pltpu.SemaphoreType.DMA((levels,)), pltpu.SemaphoreType.DMA((levels,))],
        compiler_params=pltpu.CompilerParams(collective_id=1, has_side_effects=True),
        cost_estimate=pl.CostEstimate(flops=2 * 10**10, bytes_accessed=3 * cols * strip.size, transcendentals=0),
        name="gather_strips",
    )(strip)
    return out.reshape((cols,) + strip.shape)


def reduce_kernel(levels, parts_ref, sum_ref, *scratch):
    landing, sums, (send_sem, recv_sem) = scratch[:levels], scratch[levels : 2 * levels - 1], scratch[2 * levels - 1 :]
    me = lax.axis_index("col")
    greet(me, levels)
    source = parts_ref
    for bit in range(levels):
        dim = levels - 1 - bit
        flag, partner = partner_of(me, bit)
        lead = (slice(None),) * dim
        tail = (slice(None),) * (bit + 2)
        copy = pltpu.make_async_remote_copy(
            src_ref=source.at[lead + (pl.ds(1 - flag, 1),) + tail],
            dst_ref=landing[bit],
            send_sem=send_sem.at[bit],
            recv_sem=recv_sem.at[bit],
            device_id={"col": partner},
        )
        copy.start()
        copy.wait()
        mine = source[lead + (pl.ds(flag, 1),) + tail]
        total = mine.astype(jnp.float32) + landing[bit][...].astype(jnp.float32)
        if bit < levels - 1:
            source = sums[bit]
            source[...] = total
        else:
            sum_ref[...] = total.reshape(sum_ref.shape)


def reduce_strips(parts):
    cols, rows, width = parts.shape
    levels = cols.bit_length() - 1
    vmem = pl.BlockSpec(memory_space=pltpu.VMEM)
    shapes = [(2,) * (levels - 1 - bit) + (1,) * (bit + 1) + (rows, width) for bit in range(levels)]
    return pl.pallas_call(
        functools.partial(reduce_kernel, levels),
        out_shape=jax.ShapeDtypeStruct((rows, width), jnp.float32),
        in_specs=[vmem],
        out_specs=vmem,
        scratch_shapes=[pltpu.VMEM(shape, jnp.float32 if bit else parts.dtype) for bit, shape in enumerate(shapes)]
        + [pltpu.VMEM(shape, jnp.float32) for shape in shapes[:-1]]
        + [pltpu.SemaphoreType.DMA((levels,)), pltpu.SemaphoreType.DMA((levels,))],
        compiler_params=pltpu.CompilerParams(collective_id=2, has_side_effects=True),
        cost_estimate=pl.CostEstimate(flops=2 * 10**10, bytes_accessed=3 * parts.size, transcendentals=0),
        name="reduce_strips",
    )(parts.reshape((2,) * levels + (rows, width)))


def exchange(pieces):
    return lax.all_to_all(pieces, "col", split_axis=0, concat_axis=0, tiled=True)


def body(queries, key_rows, value_rows, out_grad, dropout_bits, partner, block_pick, global_blocks):
    tokens_here, width = queries.shape
    blocks = tokens_here // BLOCK
    bands, cols = lax.axis_size("row"), lax.axis_size("col")
    band, place = lax.axis_index("row"), lax.axis_index("col")
    rows = BLOCK // cols
    part = width // CHUNKS
    size = bands * cols
    up = [(i, (i + 1) % size) for i in range(size)]
    down = [(j, i) for i, j in up]
    ordering = lax.dynamic_index_in_dim(partner, band, 1, keepdims=False)
    picks = lax.dynamic_index_in_dim(block_pick, band, 1, keepdims=False)
    col_ids = jnp.arange(cols, dtype=jnp.int32)
    hits = ordering[:, :, None] == col_ids[None, None, :]
    inverse = jnp.sum(jnp.where(hits, col_ids[None, :, None], 0), axis=1)
    asked = jnp.sum(jnp.where(hits, picks[:, :, None], 0), axis=1)
    wanted_ids = (ordering * blocks + picks).T.reshape(-1)
    band_start = band * cols * blocks
    global_ids = jnp.clip(global_blocks - band_start, 0, cols * blocks - 1)
    bits = dropout_bits.reshape(blocks, BLOCK, -1).swapaxes(1, 2)
    attended, query_grad, key_grad, value_grad = [], [], [], []
    for chunk in range(CHUNKS):
        lower, upper = chunk * part, (chunk + 1) * part
        both = jnp.concatenate([key_rows[:, lower:upper], value_rows[:, lower:upper]], 1)
        spread = exchange(both.reshape(blocks, cols, rows, 2 * part).swapaxes(0, 1))
        strips = spread.reshape(cols * blocks, rows, 2 * part)
        global_strips = jnp.take(strips, global_ids, axis=0)
        owners = global_blocks // (cols * blocks)
        chosen = global_strips
        for step in range(1, bands):
            ring = [(i, (i + step) % bands) for i in range(bands)]
            other = lax.ppermute(global_strips, "row", ring)
            chosen = jnp.where((owners == (band - step) % bands)[:, None, None], other, chosen)
        shared = gather_strips(chosen.reshape(NGLOBAL * rows, 2 * part), cols)
        shared = shared.reshape(cols, NGLOBAL, rows, 2 * part).swapaxes(0, 1).reshape(NGLOBAL * BLOCK, 2 * part)
        sent = jnp.take(strips, wanted_ids, axis=0).reshape(cols, NMATCH, rows, 2 * part)
        fetched = exchange(sent).swapaxes(0, 1).reshape(NMATCH * BLOCK, 2 * part)
        before = lax.ppermute(both[tokens_here - BLOCK :], ("row", "col"), up)
        after = lax.ppermute(both[:BLOCK], ("row", "col"), down)
        att, qgrad, own, rims, far = attention(
            queries, out_grad, key_rows, value_rows, before, after, shared, fetched, bits, chunk
        )
        attended.append(att)
        query_grad.append(qgrad)
        from_next = lax.ppermute(rims[:, :BLOCK], ("row", "col"), down)
        from_last = lax.ppermute(rims[:, BLOCK:], ("row", "col"), up)
        slots = NGLOBAL + NMATCH
        pieces = far.reshape(2, slots, cols, rows, part).transpose(2, 1, 0, 3, 4)
        landed = exchange(pieces[:, NGLOBAL:])
        strips_sum = reduce_strips(pieces[:, :NGLOBAL].reshape(cols, NGLOBAL * 2 * rows, part))
        band_sum = strips_sum.reshape(NGLOBAL, 2, rows, part)
        global_sum = band_sum
        for step in range(1, bands):
            ring = [(i, (i + step) % bands) for i in range(bands)]
            global_sum = global_sum + lax.ppermute(band_sum, "row", ring)
        block_ids = (band_start + jnp.arange(cols * blocks, dtype=jnp.int32)).reshape(cols, blocks)
        local_ids = jnp.arange(blocks, dtype=jnp.int32)
        returned = jnp.zeros((cols, blocks, 2, rows, part), jnp.float32)
        for matching in range(NMATCH):
            moved = jnp.take(landed[:, matching], inverse[matching], axis=0).astype(jnp.float32)
            mine = asked[matching][:, None] == local_ids[None, :]
            returned = returned + jnp.where(mine[:, :, None, None, None], moved[:, None], 0.0)
        for g in range(NGLOBAL):
            mine = block_ids == global_blocks[g]
            returned = returned + jnp.where(mine[:, :, None, None, None], global_sum[g][None, None], 0.0)
        home = exchange(returned.astype(jnp.bfloat16)).transpose(2, 1, 0, 3, 4).reshape(2, tokens_here, part)
        total = own + home.astype(jnp.float32)
        room = ((0, 0), (0, tokens_here - BLOCK), (0, 0))
        total = total + jnp.pad(from_last.astype(jnp.float32), room)
        total = total + jnp.pad(from_next.astype(jnp.float32), (room[0], room[1][::-1], room[2]))
        key_grad.append(total[0].astype(jnp.bfloat16))
        value_grad.append(total[1].astype(jnp.bfloat16))
    return tuple(jnp.concatenate(parts, 1) for parts in (attended, query_grad, key_grad, value_grad))


def solution(mesh):
    split = P(("row", "col"), None)
    return jax.shard_map(
        body,
        mesh=mesh,
        in_specs=(split,) * 5 + (P(),) * 3,
        out_specs=(split,) * 4,
        check_vma=False,
    )
```

```python
import functools

import jax
import jax.numpy as jnp
from jax import lax
from jax.experimental import pallas as pl
from jax.experimental.pallas import tpu as pltpu
from jax.sharding import PartitionSpec as P

HEADS = 16
HEAD_DIM = 64
BLOCK = 128
NGLOBAL = 2
NMATCH = 3
PAIR = 2 * HEAD_DIM
SLOTS = 3 + NGLOBAL + NMATCH
CHUNKS = 1

score_scale = 0.125
keep_scale = 1.0 / 0.9


def contract(a, b, dim_a, dim_b):
    return lax.dot_general(a, b, (((dim_a,), (dim_b,)), ((), ())), preferred_element_type=jnp.float32)


def attention_kernel(
    blocks, q_ref, g_ref, ko_ref, vo_ref, kp_ref, vp_ref, kn_ref, vn_ref, kg_ref, vg_ref, kr_ref, vr_ref, bits_ref,
    att_ref, qg_ref, own_ref, rims_ref, far_ref,
    keep_ref, kall_ref, vall_ref, qall_ref, gall_ref, s_ref, dp_ref, p_ref, ds_ref,
):
    near = blocks + 2
    own_rows = blocks * BLOCK

    @pl.when(pl.program_id(0) == 0)
    def _():
        shifts = lax.broadcasted_iota(jnp.int32, (BLOCK // 8, 8, BLOCK), 1)
        for j in range(blocks):
            for i in range(SLOTS):
                words = bits_ref[j, i * BLOCK // 8 : (i + 1) * BLOCK // 8, :]
                flags = jnp.right_shift(jnp.broadcast_to(words[:, None, :], shifts.shape), shifts) & 1
                keep_ref[j, i] = (flags.astype(jnp.float32) * keep_scale).reshape(BLOCK, BLOCK)
        p_ref[...] = jnp.zeros_like(p_ref)
        ds_ref[...] = jnp.zeros_like(ds_ref)

    for all_ref, parts in ((kall_ref, (kp_ref, ko_ref, kn_ref, kg_ref, kr_ref)), (vall_ref, (vp_ref, vo_ref, vn_ref, vg_ref, vr_ref))):
        row = 0
        for part in parts:
            all_ref[row : row + part.shape[0], :] = part[...]
            row += part.shape[0]
    first = lax.broadcasted_iota(jnp.int32, (BLOCK, PAIR), 1) < HEAD_DIM
    zero = jnp.zeros((BLOCK, PAIR), jnp.bfloat16)
    for j in range(blocks):
        rows = slice(j * BLOCK, (j + 1) * BLOCK)
        query = (q_ref[rows, :].astype(jnp.float32) * score_scale).astype(jnp.bfloat16)
        grad = g_ref[rows, :]
        base = 2 * j * BLOCK
        qall_ref[base : base + BLOCK, :] = jnp.where(first, query, zero)
        qall_ref[base + BLOCK : base + 2 * BLOCK, :] = jnp.where(first, zero, query)
        gall_ref[base : base + BLOCK, :] = jnp.where(first, grad, zero)
        gall_ref[base + BLOCK : base + 2 * BLOCK, :] = jnp.where(first, zero, grad)

    wide = 2 * BLOCK
    for j in range(blocks):
        cols = slice(j * wide, (j + 1) * wide)
        places = [j, j + 1, j + 2] + list(range(near, near + NGLOBAL + NMATCH))
        query = qall_ref[cols, :]
        grad = gall_ref[cols, :]
        top = None
        for i, b in enumerate(places):
            score = contract(kall_ref[b * BLOCK : (b + 1) * BLOCK, :], query, 1, 1)
            s_ref[i] = score
            part = jnp.max(score.reshape(BLOCK // 8, 8, wide), axis=0)
            top = part if top is None else jnp.maximum(top, part)
        top = jnp.max(top, axis=0, keepdims=True)
        total, mixed = None, None
        for i, b in enumerate(places):
            keep = keep_ref[j, i]
            keep = jnp.concatenate([keep, keep], axis=1)
            weight = jnp.exp(s_ref[i] - top)
            s_ref[i] = weight
            grad_p = contract(vall_ref[b * BLOCK : (b + 1) * BLOCK, :], grad, 1, 1) * keep
            dp_ref[i] = grad_p
            part = jnp.sum(weight.reshape(BLOCK // 8, 8, wide), axis=0)
            cross = jnp.sum((weight * grad_p).reshape(BLOCK // 8, 8, wide), axis=0)
            total = part if total is None else total + part
            mixed = cross if mixed is None else mixed + cross
        inverse = 1.0 / jnp.sum(total, axis=0, keepdims=True)
        delta = jnp.sum(mixed, axis=0, keepdims=True) * inverse
        for i, b in enumerate(places):
            keep = keep_ref[j, i]
            keep = jnp.concatenate([keep, keep], axis=1)
            probs = s_ref[i] * inverse
            p_ref[b * BLOCK : (b + 1) * BLOCK, cols] = (probs * keep).astype(jnp.bfloat16)
            ds_ref[b * BLOCK : (b + 1) * BLOCK, cols] = (probs * (dp_ref[i] - delta)).astype(jnp.bfloat16)

    out_t = contract(vall_ref[...], p_ref[...], 0, 0)
    qg_t = contract(kall_ref[...], ds_ref[...], 0, 0) * score_scale
    for j in range(blocks):
        rows = slice(j * BLOCK, (j + 1) * BLOCK)
        base = j * wide
        for result, ref in ((out_t, att_ref), (qg_t, qg_ref)):
            picked = jnp.concatenate(
                [result[:HEAD_DIM, base : base + BLOCK], result[HEAD_DIM:, base + BLOCK : base + wide]], axis=0
            )
            ref[rows, :] = picked.T.astype(jnp.bfloat16)
    for which, (left, right) in enumerate(((ds_ref, qall_ref), (p_ref, gall_ref))):
        grads = contract(left[...], right[...], 1, 0)
        own_ref[which] = grads[BLOCK : BLOCK + own_rows]
        rims_ref[which, :BLOCK] = grads[:BLOCK].astype(jnp.bfloat16)
        rims_ref[which, BLOCK:] = grads[BLOCK + own_rows : near * BLOCK].astype(jnp.bfloat16)
        far_ref[which] = grads[near * BLOCK :].astype(jnp.bfloat16)


def attention(queries, out_grad, key_rows, value_rows, before, after, shared, fetched, bits, chunk):
    tokens_here, width = queries.shape
    blocks = tokens_here // BLOCK
    pairs = width // PAIR // CHUNKS
    start = chunk * pairs
    part_width = width // CHUNKS
    far_rows = (NGLOBAL + NMATCH) * BLOCK
    all_rows = (blocks + 2) * BLOCK + far_rows

    def plain(rows):
        return pl.BlockSpec((rows, PAIR), lambda h: (0, start + h))

    def halves(rows):
        return [pl.BlockSpec((rows, PAIR), lambda h: (0, h)), pl.BlockSpec((rows, PAIR), lambda h: (0, pairs + h))]

    def out(rows, kind):
        return pl.BlockSpec((2, rows, PAIR), lambda h: (0, 0, h)), jax.ShapeDtypeStruct((2, rows, part_width), kind)

    flat = pl.BlockSpec((tokens_here, PAIR), lambda h: (0, h)), jax.ShapeDtypeStruct((tokens_here, part_width), jnp.bfloat16)
    outs = [flat, flat, out(tokens_here, jnp.float32), out(2 * BLOCK, jnp.bfloat16), out(far_rows, jnp.bfloat16)]
    pair_work = HEADS // CHUNKS * tokens_here * SLOTS * BLOCK
    return pl.pallas_call(
        functools.partial(attention_kernel, blocks),
        grid=(pairs,),
        in_specs=[plain(tokens_here)] * 4
        + halves(BLOCK) + halves(BLOCK) + halves(NGLOBAL * BLOCK) + halves(NMATCH * BLOCK)
        + [pl.BlockSpec(bits.shape, lambda h: (0, 0, 0))],
        out_specs=[spec for spec, _ in outs],
        out_shape=[shape for _, shape in outs],
        scratch_shapes=[
            pltpu.VMEM((blocks, SLOTS, BLOCK, BLOCK), jnp.float32),
            pltpu.VMEM((all_rows, PAIR), jnp.bfloat16),
            pltpu.VMEM((all_rows, PAIR), jnp.bfloat16),
            pltpu.VMEM((2 * tokens_here, PAIR), jnp.bfloat16),
            pltpu.VMEM((2 * tokens_here, PAIR), jnp.bfloat16),
            pltpu.VMEM((SLOTS, BLOCK, 2 * BLOCK), jnp.float32),
            pltpu.VMEM((SLOTS, BLOCK, 2 * BLOCK), jnp.float32),
            pltpu.VMEM((all_rows, 2 * tokens_here), jnp.bfloat16),
            pltpu.VMEM((all_rows, 2 * tokens_here), jnp.bfloat16),
        ],
        cost_estimate=pl.CostEstimate(
            flops=pair_work * HEAD_DIM * 2 * 7, bytes_accessed=16 * tokens_here * part_width, transcendentals=pair_work
        ),
        name="block_attention",
    )(queries, out_grad, key_rows, value_rows, before, before, after, after, shared, shared, fetched, fetched, bits)


def partner_of(me, bit):
    flag = (me // 2**bit) % 2
    return flag, me + 2**bit - 2 * 2**bit * flag


def greet(me, cols):
    barrier = pltpu.get_barrier_semaphore()

    def hello(step, carry):
        pl.semaphore_signal(barrier, inc=1, device_id={"col": (me + step) % cols})
        return carry

    lax.fori_loop(1, cols, hello, 0)
    pl.semaphore_wait(barrier, cols - 1)


def bulk_copy(me, cols, step, from_ref, to_ref, sems):
    other = (me + step) % cols
    return pltpu.make_async_remote_copy(
        src_ref=from_ref.at[other],
        dst_ref=to_ref.at[me],
        send_sem=sems[0].at[step],
        recv_sem=sems[1].at[step],
        device_id={"col": other},
    )


def bulk_start(me, cols, lower, upper, from_ref, to_ref, sems):
    def send(step, carry):
        bulk_copy(me, cols, step, from_ref, to_ref, sems).start()
        return carry

    lax.fori_loop(lower, upper, send, 0)


def bulk_wait(me, cols, from_ref, to_ref, sems):
    def finish(step, carry):
        bulk_copy(me, cols, step, from_ref, to_ref, sems).wait()
        return carry

    lax.fori_loop(1, cols, finish, 0)


def groups_of(cols, levels):
    return [1 + (cols - 1) * i // levels for i in range(levels + 1)]


def gather_kernel(cols, levels, strip_ref, from_ref, all_ref, to_ref, send_sem, recv_sem, *sems):
    me = lax.axis_index("col")
    greet(me, cols)
    flags = [partner_of(me, levels - 1 - d)[0] for d in range(levels)]
    here = tuple(pl.ds(flag, 1) for flag in flags)
    bounds = groups_of(cols, levels)
    all_ref[here] = strip_ref[...].reshape((1,) * levels + strip_ref.shape)
    for dim in range(levels):
        region = (slice(None),) * dim + here[dim:]
        copy = pltpu.make_async_remote_copy(
            src_ref=all_ref.at[region],
            dst_ref=all_ref.at[region],
            send_sem=send_sem.at[dim],
            recv_sem=recv_sem.at[dim],
            device_id={"col": partner_of(me, levels - 1 - dim)[1]},
        )
        copy.start()
        bulk_start(me, cols, bounds[dim], bounds[dim + 1], from_ref, to_ref, sems)
        if dim == 0:
            to_ref[me] = from_ref[me]
        copy.wait()
    bulk_wait(me, cols, from_ref, to_ref, sems)


def gather_exchange(strip, pieces):
    cols = pieces.shape[0]
    levels = cols.bit_length() - 1
    vmem = pl.BlockSpec(memory_space=pltpu.VMEM)
    out, landed = pl.pallas_call(
        functools.partial(gather_kernel, cols, levels),
        out_shape=[
            jax.ShapeDtypeStruct((2,) * levels + strip.shape, strip.dtype),
            jax.ShapeDtypeStruct(pieces.shape, pieces.dtype),
        ],
        in_specs=[vmem, vmem],
        out_specs=[vmem, vmem],
        scratch_shapes=[pltpu.SemaphoreType.DMA((levels,))] * 2 + [pltpu.SemaphoreType.DMA((cols,))] * 2,
        compiler_params=pltpu.CompilerParams(collective_id=1, has_side_effects=True),
        cost_estimate=pl.CostEstimate(flops=3 * 10**10, bytes_accessed=4 * pieces.size, transcendentals=0),
        name="gather_exchange",
    )(strip, pieces)
    return out.reshape((cols,) + strip.shape), landed


def reduce_kernel(cols, levels, parts_ref, from_ref, sum_ref, to_ref, *scratch):
    landing, sums = scratch[:levels], scratch[levels : 2 * levels - 1]
    send_sem, recv_sem = scratch[2 * levels - 1 : 2 * levels + 1]
    sems = scratch[2 * levels + 1 :]
    me = lax.axis_index("col")
    greet(me, cols)
    bounds = groups_of(cols, levels)
    source = parts_ref
    for bit in range(levels):
        dim = levels - 1 - bit
        flag, partner = partner_of(me, bit)
        lead = (slice(None),) * dim
        tail = (slice(None),) * (bit + 2)
        copy = pltpu.make_async_remote_copy(
            src_ref=source.at[lead + (pl.ds(1 - flag, 1),) + tail],
            dst_ref=landing[bit],
            send_sem=send_sem.at[bit],
            recv_sem=recv_sem.at[bit],
            device_id={"col": partner},
        )
        copy.start()
        bulk_start(me, cols, bounds[bit], bounds[bit + 1], from_ref, to_ref, sems)
        if bit == 0:
            to_ref[me] = from_ref[me]
        copy.wait()
        mine = source[lead + (pl.ds(flag, 1),) + tail]
        total = mine.astype(jnp.float32) + landing[bit][...].astype(jnp.float32)
        if bit < levels - 1:
            source = sums[bit]
            source[...] = total
        else:
            sum_ref[...] = total.reshape(sum_ref.shape)
    bulk_wait(me, cols, from_ref, to_ref, sems)


def reduce_exchange(parts, pieces):
    cols, rows, width = parts.shape
    levels = cols.bit_length() - 1
    vmem = pl.BlockSpec(memory_space=pltpu.VMEM)
    shapes = [(2,) * (levels - 1 - bit) + (1,) * (bit + 1) + (rows, width) for bit in range(levels)]
    return pl.pallas_call(
        functools.partial(reduce_kernel, cols, levels),
        out_shape=[
            jax.ShapeDtypeStruct((rows, width), jnp.float32),
            jax.ShapeDtypeStruct(pieces.shape, pieces.dtype),
        ],
        in_specs=[vmem, vmem],
        out_specs=[vmem, vmem],
        scratch_shapes=[pltpu.VMEM(shape, jnp.float32 if bit else parts.dtype) for bit, shape in enumerate(shapes)]
        + [pltpu.VMEM(shape, jnp.float32) for shape in shapes[:-1]]
        + [pltpu.SemaphoreType.DMA((levels,))] * 2 + [pltpu.SemaphoreType.DMA((cols,))] * 2,
        compiler_params=pltpu.CompilerParams(collective_id=2, has_side_effects=True),
        cost_estimate=pl.CostEstimate(flops=3 * 10**10, bytes_accessed=4 * pieces.size, transcendentals=0),
        name="reduce_exchange",
    )(parts.reshape((2,) * levels + (rows, width)), pieces)


def exchange(pieces):
    return lax.all_to_all(pieces, "col", split_axis=0, concat_axis=0, tiled=True)


def body(queries, key_rows, value_rows, out_grad, dropout_bits, partner, block_pick, global_blocks):
    tokens_here, width = queries.shape
    blocks = tokens_here // BLOCK
    bands, cols = lax.axis_size("row"), lax.axis_size("col")
    band, place = lax.axis_index("row"), lax.axis_index("col")
    rows = BLOCK // cols
    part = width // CHUNKS
    size = bands * cols
    up = [(i, (i + 1) % size) for i in range(size)]
    down = [(j, i) for i, j in up]
    ordering = lax.dynamic_index_in_dim(partner, band, 1, keepdims=False)
    picks = lax.dynamic_index_in_dim(block_pick, band, 1, keepdims=False)
    col_ids = jnp.arange(cols, dtype=jnp.int32)
    hits = ordering[:, :, None] == col_ids[None, None, :]
    inverse = jnp.sum(jnp.where(hits, col_ids[None, :, None], 0), axis=1)
    asked = jnp.sum(jnp.where(hits, picks[:, :, None], 0), axis=1)
    wanted_ids = (ordering * blocks + picks).T.reshape(-1)
    band_start = band * cols * blocks
    global_ids = jnp.clip(global_blocks - band_start, 0, cols * blocks - 1)
    bits = dropout_bits.reshape(blocks, BLOCK, -1).swapaxes(1, 2)
    attended, query_grad, key_grad, value_grad = [], [], [], []
    for chunk in range(CHUNKS):
        lower, upper = chunk * part, (chunk + 1) * part
        both = jnp.concatenate([key_rows[:, lower:upper], value_rows[:, lower:upper]], 1)
        spread = exchange(both.reshape(blocks, cols, rows, 2 * part).swapaxes(0, 1))
        strips = spread.reshape(cols * blocks, rows, 2 * part)
        global_strips = jnp.take(strips, global_ids, axis=0)
        owners = global_blocks // (cols * blocks)
        chosen = global_strips
        for step in range(1, bands):
            ring = [(i, (i + step) % bands) for i in range(bands)]
            other = lax.ppermute(global_strips, "row", ring)
            chosen = jnp.where((owners == (band - step) % bands)[:, None, None], other, chosen)
        sent = jnp.take(strips, wanted_ids, axis=0).reshape(cols, NMATCH, rows, 2 * part)
        shared, fetched = gather_exchange(
            chosen.reshape(NGLOBAL * rows, 2 * part), sent.reshape(cols, NMATCH * rows, 2 * part)
        )
        shared = shared.reshape(cols, NGLOBAL, rows, 2 * part).swapaxes(0, 1).reshape(NGLOBAL * BLOCK, 2 * part)
        fetched = fetched.reshape(cols, NMATCH, rows, 2 * part)
        fetched = fetched.swapaxes(0, 1).reshape(NMATCH * BLOCK, 2 * part)
        before = lax.ppermute(both[tokens_here - BLOCK :], ("row", "col"), up)
        after = lax.ppermute(both[:BLOCK], ("row", "col"), down)
        att, qgrad, own, rims, far = attention(
            queries, out_grad, key_rows, value_rows, before, after, shared, fetched, bits, chunk
        )
        attended.append(att)
        query_grad.append(qgrad)
        from_next = lax.ppermute(rims[:, :BLOCK], ("row", "col"), down)
        from_last = lax.ppermute(rims[:, BLOCK:], ("row", "col"), up)
        slots = NGLOBAL + NMATCH
        pieces = far.reshape(2, slots, cols, rows, part).transpose(2, 1, 0, 3, 4)
        strips_sum, landed = reduce_exchange(
            pieces[:, :NGLOBAL].reshape(cols, NGLOBAL * 2 * rows, part),
            pieces[:, NGLOBAL:].reshape(cols, NMATCH * 2 * rows, part),
        )
        landed = landed.reshape(cols, NMATCH, 2, rows, part)
        band_sum = strips_sum.reshape(NGLOBAL, 2, rows, part)
        global_sum = band_sum
        for step in range(1, bands):
            ring = [(i, (i + step) % bands) for i in range(bands)]
            global_sum = global_sum + lax.ppermute(band_sum, "row", ring)
        block_ids = (band_start + jnp.arange(cols * blocks, dtype=jnp.int32)).reshape(cols, blocks)
        local_ids = jnp.arange(blocks, dtype=jnp.int32)
        returned = jnp.zeros((cols, blocks, 2, rows, part), jnp.float32)
        for matching in range(NMATCH):
            moved = jnp.take(landed[:, matching], inverse[matching], axis=0).astype(jnp.float32)
            mine = asked[matching][:, None] == local_ids[None, :]
            returned = returned + jnp.where(mine[:, :, None, None, None], moved[:, None], 0.0)
        for g in range(NGLOBAL):
            mine = block_ids == global_blocks[g]
            returned = returned + jnp.where(mine[:, :, None, None, None], global_sum[g][None, None], 0.0)
        home = exchange(returned.astype(jnp.bfloat16)).transpose(2, 1, 0, 3, 4).reshape(2, tokens_here, part)
        total = own + home.astype(jnp.float32)
        room = ((0, 0), (0, tokens_here - BLOCK), (0, 0))
        total = total + jnp.pad(from_last.astype(jnp.float32), room)
        total = total + jnp.pad(from_next.astype(jnp.float32), (room[0], room[1][::-1], room[2]))
        key_grad.append(total[0].astype(jnp.bfloat16))
        value_grad.append(total[1].astype(jnp.bfloat16))
    return tuple(jnp.concatenate(parts, 1) for parts in (attended, query_grad, key_grad, value_grad))


def solution(mesh):
    split = P(("row", "col"), None)
    return jax.shard_map(
        body,
        mesh=mesh,
        in_specs=(split,) * 5 + (P(),) * 3,
        out_specs=(split,) * 4,
        check_vma=False,
    )
```

```python
import functools

import jax
import jax.numpy as jnp
from jax import lax
from jax.experimental import pallas as pl
from jax.experimental.pallas import tpu as pltpu
from jax.sharding import PartitionSpec as P

HEADS = 16
HEAD_DIM = 64
BLOCK = 128
NGLOBAL = 2
NMATCH = 3
PAIR = 2 * HEAD_DIM
SLOTS = 3 + NGLOBAL + NMATCH
CHUNKS = 1

score_scale = 0.125
keep_scale = 1.0 / 0.9


def contract(a, b, dim_a, dim_b):
    return lax.dot_general(a, b, (((dim_a,), (dim_b,)), ((), ())), preferred_element_type=jnp.float32)


def attention_kernel(
    blocks, q_ref, g_ref, ko_ref, vo_ref, kp_ref, vp_ref, kn_ref, vn_ref, kg_ref, vg_ref, kr_ref, vr_ref, bits_ref,
    att_ref, qg_ref, own_ref, rims_ref, far_ref,
    keep_ref, kall_ref, vall_ref, qall_ref, gall_ref, s_ref, dp_ref, p_ref, ds_ref,
):
    near = blocks + 2
    own_rows = blocks * BLOCK

    @pl.when(pl.program_id(0) == 0)
    def _():
        shifts = lax.broadcasted_iota(jnp.int32, (BLOCK // 8, 8, BLOCK), 1)
        for j in range(blocks):
            for i in range(SLOTS):
                words = bits_ref[j, i * BLOCK // 8 : (i + 1) * BLOCK // 8, :]
                flags = jnp.right_shift(jnp.broadcast_to(words[:, None, :], shifts.shape), shifts) & 1
                keep_ref[j, i] = (flags.astype(jnp.float32) * keep_scale).reshape(BLOCK, BLOCK)
        p_ref[...] = jnp.zeros_like(p_ref)
        ds_ref[...] = jnp.zeros_like(ds_ref)

    for all_ref, parts in ((kall_ref, (kp_ref, ko_ref, kn_ref, kg_ref, kr_ref)), (vall_ref, (vp_ref, vo_ref, vn_ref, vg_ref, vr_ref))):
        row = 0
        for part in parts:
            all_ref[row : row + part.shape[0], :] = part[...]
            row += part.shape[0]
    first = lax.broadcasted_iota(jnp.int32, (BLOCK, PAIR), 1) < HEAD_DIM
    zero = jnp.zeros((BLOCK, PAIR), jnp.bfloat16)
    for j in range(blocks):
        rows = slice(j * BLOCK, (j + 1) * BLOCK)
        query = (q_ref[rows, :].astype(jnp.float32) * score_scale).astype(jnp.bfloat16)
        grad = g_ref[rows, :]
        base = 2 * j * BLOCK
        qall_ref[base : base + BLOCK, :] = jnp.where(first, query, zero)
        qall_ref[base + BLOCK : base + 2 * BLOCK, :] = jnp.where(first, zero, query)
        gall_ref[base : base + BLOCK, :] = jnp.where(first, grad, zero)
        gall_ref[base + BLOCK : base + 2 * BLOCK, :] = jnp.where(first, zero, grad)

    wide = 2 * BLOCK
    for j in range(blocks):
        cols = slice(j * wide, (j + 1) * wide)
        places = [j, j + 1, j + 2] + list(range(near, near + NGLOBAL + NMATCH))
        query = qall_ref[cols, :]
        grad = gall_ref[cols, :]
        top = None
        for i, b in enumerate(places):
            score = contract(kall_ref[b * BLOCK : (b + 1) * BLOCK, :], query, 1, 1)
            s_ref[i] = score
            part = jnp.max(score.reshape(BLOCK // 8, 8, wide), axis=0)
            top = part if top is None else jnp.maximum(top, part)
        top = jnp.max(top, axis=0, keepdims=True)
        total, mixed = None, None
        for i, b in enumerate(places):
            keep = keep_ref[j, i]
            keep = jnp.concatenate([keep, keep], axis=1)
            weight = jnp.exp(s_ref[i] - top)
            s_ref[i] = weight
            grad_p = contract(vall_ref[b * BLOCK : (b + 1) * BLOCK, :], grad, 1, 1) * keep
            dp_ref[i] = grad_p
            part = jnp.sum(weight.reshape(BLOCK // 8, 8, wide), axis=0)
            cross = jnp.sum((weight * grad_p).reshape(BLOCK // 8, 8, wide), axis=0)
            total = part if total is None else total + part
            mixed = cross if mixed is None else mixed + cross
        inverse = 1.0 / jnp.sum(total, axis=0, keepdims=True)
        delta = jnp.sum(mixed, axis=0, keepdims=True) * inverse
        for i, b in enumerate(places):
            keep = keep_ref[j, i]
            keep = jnp.concatenate([keep, keep], axis=1)
            probs = s_ref[i] * inverse
            p_ref[b * BLOCK : (b + 1) * BLOCK, cols] = (probs * keep).astype(jnp.bfloat16)
            ds_ref[b * BLOCK : (b + 1) * BLOCK, cols] = (probs * (dp_ref[i] - delta)).astype(jnp.bfloat16)

    out_t = contract(vall_ref[...], p_ref[...], 0, 0)
    qg_t = contract(kall_ref[...], ds_ref[...], 0, 0) * score_scale
    for j in range(blocks):
        rows = slice(j * BLOCK, (j + 1) * BLOCK)
        base = j * wide
        for result, ref in ((out_t, att_ref), (qg_t, qg_ref)):
            picked = jnp.concatenate(
                [result[:HEAD_DIM, base : base + BLOCK], result[HEAD_DIM:, base + BLOCK : base + wide]], axis=0
            )
            ref[rows, :] = picked.T.astype(jnp.bfloat16)
    for which, (left, right) in enumerate(((ds_ref, qall_ref), (p_ref, gall_ref))):
        grads = contract(left[...], right[...], 1, 0)
        own_ref[which] = grads[BLOCK : BLOCK + own_rows]
        rims_ref[which, :BLOCK] = grads[:BLOCK].astype(jnp.bfloat16)
        rims_ref[which, BLOCK:] = grads[BLOCK + own_rows : near * BLOCK].astype(jnp.bfloat16)
        far_ref[which] = grads[near * BLOCK :].astype(jnp.bfloat16)


def attention(queries, out_grad, key_rows, value_rows, before, after, shared, fetched, bits, chunk):
    tokens_here, width = queries.shape
    blocks = tokens_here // BLOCK
    pairs = width // PAIR // CHUNKS
    start = chunk * pairs
    part_width = width // CHUNKS
    far_rows = (NGLOBAL + NMATCH) * BLOCK
    all_rows = (blocks + 2) * BLOCK + far_rows

    def plain(rows):
        return pl.BlockSpec((rows, PAIR), lambda h: (0, start + h))

    def halves(rows):
        return [pl.BlockSpec((rows, PAIR), lambda h: (0, h)), pl.BlockSpec((rows, PAIR), lambda h: (0, pairs + h))]

    def out(rows, kind):
        return pl.BlockSpec((2, rows, PAIR), lambda h: (0, 0, h)), jax.ShapeDtypeStruct((2, rows, part_width), kind)

    flat = pl.BlockSpec((tokens_here, PAIR), lambda h: (0, h)), jax.ShapeDtypeStruct((tokens_here, part_width), jnp.bfloat16)
    outs = [flat, flat, out(tokens_here, jnp.float32), out(2 * BLOCK, jnp.bfloat16), out(far_rows, jnp.bfloat16)]
    pair_work = HEADS // CHUNKS * tokens_here * SLOTS * BLOCK
    return pl.pallas_call(
        functools.partial(attention_kernel, blocks),
        grid=(pairs,),
        in_specs=[plain(tokens_here)] * 4
        + halves(BLOCK) + halves(BLOCK) + halves(NGLOBAL * BLOCK) + halves(NMATCH * BLOCK)
        + [pl.BlockSpec(bits.shape, lambda h: (0, 0, 0))],
        out_specs=[spec for spec, _ in outs],
        out_shape=[shape for _, shape in outs],
        scratch_shapes=[
            pltpu.VMEM((blocks, SLOTS, BLOCK, BLOCK), jnp.float32),
            pltpu.VMEM((all_rows, PAIR), jnp.bfloat16),
            pltpu.VMEM((all_rows, PAIR), jnp.bfloat16),
            pltpu.VMEM((2 * tokens_here, PAIR), jnp.bfloat16),
            pltpu.VMEM((2 * tokens_here, PAIR), jnp.bfloat16),
            pltpu.VMEM((SLOTS, BLOCK, 2 * BLOCK), jnp.float32),
            pltpu.VMEM((SLOTS, BLOCK, 2 * BLOCK), jnp.float32),
            pltpu.VMEM((all_rows, 2 * tokens_here), jnp.bfloat16),
            pltpu.VMEM((all_rows, 2 * tokens_here), jnp.bfloat16),
        ],
        cost_estimate=pl.CostEstimate(
            flops=pair_work * HEAD_DIM * 2 * 7, bytes_accessed=16 * tokens_here * part_width, transcendentals=pair_work
        ),
        name="block_attention",
    )(queries, out_grad, key_rows, value_rows, before, before, after, after, shared, shared, fetched, fetched, bits)


def partner_of(me, bit):
    flag = (me // 2**bit) % 2
    return flag, me + 2**bit - 2 * 2**bit * flag


def greet(me, cols):
    barrier = pltpu.get_barrier_semaphore()

    def hello(step, carry):
        pl.semaphore_signal(barrier, inc=1, device_id={"col": (me + step) % cols})
        return carry

    lax.fori_loop(1, cols, hello, 0)
    pl.semaphore_wait(barrier, cols - 1)


def bulk_copy(me, cols, turn, from_ref, to_ref, sems):
    step = (turn * (cols // 2 - 1)) % cols
    other = (me + step) % cols
    return pltpu.make_async_remote_copy(
        src_ref=from_ref.at[other],
        dst_ref=to_ref.at[me],
        send_sem=sems[0].at[step],
        recv_sem=sems[1].at[step],
        device_id={"col": other},
    )


def bulk_start(me, cols, lower, upper, from_ref, to_ref, sems):
    def send(step, carry):
        bulk_copy(me, cols, step, from_ref, to_ref, sems).start()
        return carry

    lax.fori_loop(lower, upper, send, 0)


def bulk_wait(me, cols, from_ref, to_ref, sems):
    def finish(step, carry):
        bulk_copy(me, cols, step, from_ref, to_ref, sems).wait()
        return carry

    lax.fori_loop(1, cols, finish, 0)


def groups_of(cols, levels):
    return [1 + (cols - 1) * i // levels for i in range(levels + 1)]


def late_groups(cols, levels):
    third, half = 1 + (cols - 1) // 3, 1 + (cols - 1) * 8 // 15
    return [1, third, third] + [half] * (levels - 3) + [cols] * 1


def exchange_kernel(cols, from_ref, to_ref, *sems):
    me = lax.axis_index("col")
    greet(me, cols)
    bulk_start(me, cols, 1, cols, from_ref, to_ref, sems)
    to_ref[me] = from_ref[me]
    bulk_wait(me, cols, from_ref, to_ref, sems)


def direct_exchange(pieces, number):
    cols = pieces.shape[0]
    vmem = pl.BlockSpec(memory_space=pltpu.VMEM)
    return pl.pallas_call(
        functools.partial(exchange_kernel, cols),
        out_shape=jax.ShapeDtypeStruct(pieces.shape, pieces.dtype),
        in_specs=[vmem],
        out_specs=vmem,
        scratch_shapes=[pltpu.SemaphoreType.DMA((cols,))] * 2,
        compiler_params=pltpu.CompilerParams(collective_id=number, has_side_effects=True),
        cost_estimate=pl.CostEstimate(flops=3 * 10**10, bytes_accessed=4 * pieces.size, transcendentals=0),
        name="direct_exchange",
    )(pieces)


def gather_kernel(cols, levels, strip_ref, from_ref, all_ref, to_ref, send_sem, recv_sem, *sems):
    me = lax.axis_index("col")
    greet(me, cols)
    flags = [partner_of(me, levels - 1 - d)[0] for d in range(levels)]
    here = tuple(pl.ds(flag, 1) for flag in flags)
    bounds = groups_of(cols, levels)
    all_ref[here] = strip_ref[...].reshape((1,) * levels + strip_ref.shape)
    for dim in range(levels):
        region = (slice(None),) * dim + here[dim:]
        copy = pltpu.make_async_remote_copy(
            src_ref=all_ref.at[region],
            dst_ref=all_ref.at[region],
            send_sem=send_sem.at[dim],
            recv_sem=recv_sem.at[dim],
            device_id={"col": partner_of(me, levels - 1 - dim)[1]},
        )
        copy.start()
        bulk_start(me, cols, bounds[dim], bounds[dim + 1], from_ref, to_ref, sems)
        if dim == 0:
            to_ref[me] = from_ref[me]
        copy.wait()
    bulk_wait(me, cols, from_ref, to_ref, sems)


def gather_exchange(strip, pieces):
    cols = pieces.shape[0]
    levels = cols.bit_length() - 1
    vmem = pl.BlockSpec(memory_space=pltpu.VMEM)
    out, landed = pl.pallas_call(
        functools.partial(gather_kernel, cols, levels),
        out_shape=[
            jax.ShapeDtypeStruct((2,) * levels + strip.shape, strip.dtype),
            jax.ShapeDtypeStruct(pieces.shape, pieces.dtype),
        ],
        in_specs=[vmem, vmem],
        out_specs=[vmem, vmem],
        scratch_shapes=[pltpu.SemaphoreType.DMA((levels,))] * 2 + [pltpu.SemaphoreType.DMA((cols,))] * 2,
        compiler_params=pltpu.CompilerParams(collective_id=1, has_side_effects=True),
        cost_estimate=pl.CostEstimate(flops=3 * 10**10, bytes_accessed=4 * pieces.size, transcendentals=0),
        name="gather_exchange",
    )(strip, pieces)
    return out.reshape((cols,) + strip.shape), landed


def reduce_kernel(cols, levels, parts_ref, from_ref, sum_ref, to_ref, *scratch):
    landing, sums = scratch[:levels], scratch[levels : 2 * levels - 1]
    send_sem, recv_sem = scratch[2 * levels - 1 : 2 * levels + 1]
    sems = scratch[2 * levels + 1 :]
    me = lax.axis_index("col")
    greet(me, cols)
    bounds = late_groups(cols, levels)
    source = parts_ref
    for bit in range(levels):
        dim = levels - 1 - bit
        flag, partner = partner_of(me, bit)
        lead = (slice(None),) * dim
        tail = (slice(None),) * (bit + 2)
        copy = pltpu.make_async_remote_copy(
            src_ref=source.at[lead + (pl.ds(1 - flag, 1),) + tail],
            dst_ref=landing[bit],
            send_sem=send_sem.at[bit],
            recv_sem=recv_sem.at[bit],
            device_id={"col": partner},
        )
        copy.start()
        bulk_start(me, cols, bounds[bit], bounds[bit + 1], from_ref, to_ref, sems)
        if bit == 0:
            to_ref[me] = from_ref[me]
        copy.wait()
        mine = source[lead + (pl.ds(flag, 1),) + tail]
        total = mine.astype(jnp.float32) + landing[bit][...].astype(jnp.float32)
        if bit < levels - 1:
            source = sums[bit]
            source[...] = total.astype(source.dtype)
        else:
            sum_ref[...] = total.reshape(sum_ref.shape)
    bulk_wait(me, cols, from_ref, to_ref, sems)


def reduce_exchange(parts, pieces):
    cols, rows, width = parts.shape
    levels = cols.bit_length() - 1
    vmem = pl.BlockSpec(memory_space=pltpu.VMEM)
    shapes = [(2,) * (levels - 1 - bit) + (1,) * (bit + 1) + (rows, width) for bit in range(levels)]
    return pl.pallas_call(
        functools.partial(reduce_kernel, cols, levels),
        out_shape=[
            jax.ShapeDtypeStruct((rows, width), jnp.float32),
            jax.ShapeDtypeStruct(pieces.shape, pieces.dtype),
        ],
        in_specs=[vmem, vmem],
        out_specs=[vmem, vmem],
        scratch_shapes=[pltpu.VMEM(shape, parts.dtype if bit < 2 else jnp.float32) for bit, shape in enumerate(shapes)]
        + [pltpu.VMEM(shape, jnp.float32 if bit else parts.dtype) for bit, shape in enumerate(shapes[:-1])]
        + [pltpu.SemaphoreType.DMA((levels,))] * 2 + [pltpu.SemaphoreType.DMA((cols,))] * 2,
        compiler_params=pltpu.CompilerParams(collective_id=2, has_side_effects=True),
        cost_estimate=pl.CostEstimate(flops=3 * 10**10, bytes_accessed=4 * pieces.size, transcendentals=0),
        name="reduce_exchange",
    )(parts.reshape((2,) * levels + (rows, width)), pieces)


def body(queries, key_rows, value_rows, out_grad, dropout_bits, partner, block_pick, global_blocks):
    tokens_here, width = queries.shape
    blocks = tokens_here // BLOCK
    bands, cols = lax.axis_size("row"), lax.axis_size("col")
    band, place = lax.axis_index("row"), lax.axis_index("col")
    rows = BLOCK // cols
    part = width // CHUNKS
    size = bands * cols
    up = [(i, (i + 1) % size) for i in range(size)]
    down = [(j, i) for i, j in up]
    ordering = lax.dynamic_index_in_dim(partner, band, 1, keepdims=False)
    picks = lax.dynamic_index_in_dim(block_pick, band, 1, keepdims=False)
    col_ids = jnp.arange(cols, dtype=jnp.int32)
    hits = ordering[:, :, None] == col_ids[None, None, :]
    inverse = jnp.sum(jnp.where(hits, col_ids[None, :, None], 0), axis=1)
    asked = jnp.sum(jnp.where(hits, picks[:, :, None], 0), axis=1)
    wanted_ids = (ordering * blocks + picks).T.reshape(-1)
    band_start = band * cols * blocks
    global_ids = jnp.clip(global_blocks - band_start, 0, cols * blocks - 1)
    bits = dropout_bits.reshape(blocks, BLOCK, -1).swapaxes(1, 2)
    attended, query_grad, key_grad, value_grad = [], [], [], []
    for chunk in range(CHUNKS):
        lower, upper = chunk * part, (chunk + 1) * part
        both = jnp.concatenate([key_rows[:, lower:upper], value_rows[:, lower:upper]], 1)
        own_strips = both.reshape(blocks, cols, rows, 2 * part).swapaxes(0, 1)
        spread = direct_exchange(own_strips.reshape(cols, blocks * rows, 2 * part), 3)
        strips = spread.reshape(cols * blocks, rows, 2 * part)
        global_strips = jnp.take(strips, global_ids, axis=0)
        owners = global_blocks // (cols * blocks)
        chosen = global_strips
        for step in range(1, bands):
            ring = [(i, (i + step) % bands) for i in range(bands)]
            other = lax.ppermute(global_strips, "row", ring)
            chosen = jnp.where((owners == (band - step) % bands)[:, None, None], other, chosen)
        sent = jnp.take(strips, wanted_ids, axis=0).reshape(cols, NMATCH, rows, 2 * part)
        shared, fetched = gather_exchange(
            chosen.reshape(NGLOBAL * rows, 2 * part), sent.reshape(cols, NMATCH * rows, 2 * part)
        )
        shared = shared.reshape(cols, NGLOBAL, rows, 2 * part).swapaxes(0, 1).reshape(NGLOBAL * BLOCK, 2 * part)
        fetched = fetched.reshape(cols, NMATCH, rows, 2 * part)
        fetched = fetched.swapaxes(0, 1).reshape(NMATCH * BLOCK, 2 * part)
        before = lax.ppermute(both[tokens_here - BLOCK :], ("row", "col"), up)
        after = lax.ppermute(both[:BLOCK], ("row", "col"), down)
        att, qgrad, own, rims, far = attention(
            queries, out_grad, key_rows, value_rows, before, after, shared, fetched, bits, chunk
        )
        attended.append(att)
        query_grad.append(qgrad)
        from_next = lax.ppermute(rims[:, :BLOCK], ("row", "col"), down)
        from_last = lax.ppermute(rims[:, BLOCK:], ("row", "col"), up)
        slots = NGLOBAL + NMATCH
        pieces = far.reshape(2, slots, cols, rows, part).transpose(2, 1, 0, 3, 4)
        strips_sum, landed = reduce_exchange(
            pieces[:, :NGLOBAL].reshape(cols, NGLOBAL * 2 * rows, part),
            pieces[:, NGLOBAL:].reshape(cols, NMATCH * 2 * rows, part),
        )
        landed = landed.reshape(cols, NMATCH, 2, rows, part)
        band_sum = strips_sum.reshape(NGLOBAL, 2, rows, part)
        global_sum = band_sum
        for step in range(1, bands):
            ring = [(i, (i + step) % bands) for i in range(bands)]
            global_sum = global_sum + lax.ppermute(band_sum, "row", ring)
        block_ids = (band_start + jnp.arange(cols * blocks, dtype=jnp.int32)).reshape(cols, blocks)
        local_ids = jnp.arange(blocks, dtype=jnp.int32)
        returned = jnp.zeros((cols, blocks, 2, rows, part), jnp.float32)
        for matching in range(NMATCH):
            moved = jnp.take(landed[:, matching], inverse[matching], axis=0).astype(jnp.float32)
            mine = asked[matching][:, None] == local_ids[None, :]
            returned = returned + jnp.where(mine[:, :, None, None, None], moved[:, None], 0.0)
        for g in range(NGLOBAL):
            mine = block_ids == global_blocks[g]
            returned = returned + jnp.where(mine[:, :, None, None, None], global_sum[g][None, None], 0.0)
        home = direct_exchange(returned.astype(jnp.bfloat16).reshape(cols, blocks * 2 * rows, part), 4)
        home = home.reshape(cols, blocks, 2, rows, part).transpose(2, 1, 0, 3, 4).reshape(2, tokens_here, part)
        total = own + home.astype(jnp.float32)
        room = ((0, 0), (0, tokens_here - BLOCK), (0, 0))
        total = total + jnp.pad(from_last.astype(jnp.float32), room)
        total = total + jnp.pad(from_next.astype(jnp.float32), (room[0], room[1][::-1], room[2]))
        key_grad.append(total[0].astype(jnp.bfloat16))
        value_grad.append(total[1].astype(jnp.bfloat16))
    return tuple(jnp.concatenate(parts, 1) for parts in (attended, query_grad, key_grad, value_grad))


def solution(mesh):
    split = P(("row", "col"), None)
    return jax.shard_map(
        body,
        mesh=mesh,
        in_specs=(split,) * 5 + (P(),) * 3,
        out_specs=(split,) * 4,
        check_vma=False,
    )
```

```python
import functools

import jax
import jax.numpy as jnp
from jax import lax
from jax.experimental import pallas as pl
from jax.experimental.pallas import tpu as pltpu
from jax.sharding import PartitionSpec as P

HEADS = 16
HEAD_DIM = 64
BLOCK = 128
NGLOBAL = 2
NMATCH = 3
PAIR = 2 * HEAD_DIM
SLOTS = 3 + NGLOBAL + NMATCH
CHUNKS = 1

score_scale = 0.125
keep_scale = 1.0 / 0.9


def contract(a, b, dim_a, dim_b):
    return lax.dot_general(a, b, (((dim_a,), (dim_b,)), ((), ())), preferred_element_type=jnp.float32)


def attention_kernel(
    blocks, q_ref, g_ref, ko_ref, vo_ref, kp_ref, vp_ref, kn_ref, vn_ref, kg_ref, vg_ref, kr_ref, vr_ref, bits_ref,
    att_ref, qg_ref, own_ref, rims_ref, far_ref,
    keep_ref, kall_ref, vall_ref, qall_ref, gall_ref, s_ref, dp_ref, p_ref, ds_ref,
):
    near = blocks + 2
    own_rows = blocks * BLOCK

    @pl.when(pl.program_id(0) == 0)
    def _():
        shifts = lax.broadcasted_iota(jnp.int32, (BLOCK // 8, 8, BLOCK), 1)
        for j in range(blocks):
            for i in range(SLOTS):
                words = bits_ref[j, i * BLOCK // 8 : (i + 1) * BLOCK // 8, :]
                flags = jnp.right_shift(jnp.broadcast_to(words[:, None, :], shifts.shape), shifts) & 1
                keep_ref[j, i] = (flags.astype(jnp.float32) * keep_scale).reshape(BLOCK, BLOCK)
        p_ref[...] = jnp.zeros_like(p_ref)
        ds_ref[...] = jnp.zeros_like(ds_ref)

    for all_ref, parts in ((kall_ref, (kp_ref, ko_ref, kn_ref, kg_ref, kr_ref)), (vall_ref, (vp_ref, vo_ref, vn_ref, vg_ref, vr_ref))):
        row = 0
        for part in parts:
            all_ref[row : row + part.shape[0], :] = part[...]
            row += part.shape[0]
    first = lax.broadcasted_iota(jnp.int32, (BLOCK, PAIR), 1) < HEAD_DIM
    zero = jnp.zeros((BLOCK, PAIR), jnp.bfloat16)
    for j in range(blocks):
        rows = slice(j * BLOCK, (j + 1) * BLOCK)
        query = (q_ref[rows, :].astype(jnp.float32) * score_scale).astype(jnp.bfloat16)
        grad = g_ref[rows, :]
        base = 2 * j * BLOCK
        qall_ref[base : base + BLOCK, :] = jnp.where(first, query, zero)
        qall_ref[base + BLOCK : base + 2 * BLOCK, :] = jnp.where(first, zero, query)
        gall_ref[base : base + BLOCK, :] = jnp.where(first, grad, zero)
        gall_ref[base + BLOCK : base + 2 * BLOCK, :] = jnp.where(first, zero, grad)

    wide = 2 * BLOCK
    for j in range(blocks):
        cols = slice(j * wide, (j + 1) * wide)
        places = [j, j + 1, j + 2] + list(range(near, near + NGLOBAL + NMATCH))
        query = qall_ref[cols, :]
        grad = gall_ref[cols, :]
        top = None
        for i, b in enumerate(places):
            score = contract(kall_ref[b * BLOCK : (b + 1) * BLOCK, :], query, 1, 1)
            s_ref[i] = score
            part = jnp.max(score.reshape(BLOCK // 8, 8, wide), axis=0)
            top = part if top is None else jnp.maximum(top, part)
        top = jnp.max(top, axis=0, keepdims=True)
        total, mixed = None, None
        for i, b in enumerate(places):
            keep = keep_ref[j, i]
            keep = jnp.concatenate([keep, keep], axis=1)
            weight = jnp.exp(s_ref[i] - top)
            s_ref[i] = weight
            grad_p = contract(vall_ref[b * BLOCK : (b + 1) * BLOCK, :], grad, 1, 1) * keep
            dp_ref[i] = grad_p
            part = jnp.sum(weight.reshape(BLOCK // 8, 8, wide), axis=0)
            cross = jnp.sum((weight * grad_p).reshape(BLOCK // 8, 8, wide), axis=0)
            total = part if total is None else total + part
            mixed = cross if mixed is None else mixed + cross
        inverse = 1.0 / jnp.sum(total, axis=0, keepdims=True)
        delta = jnp.sum(mixed, axis=0, keepdims=True) * inverse
        for i, b in enumerate(places):
            keep = keep_ref[j, i]
            keep = jnp.concatenate([keep, keep], axis=1)
            probs = s_ref[i] * inverse
            p_ref[b * BLOCK : (b + 1) * BLOCK, cols] = (probs * keep).astype(jnp.bfloat16)
            ds_ref[b * BLOCK : (b + 1) * BLOCK, cols] = (probs * (dp_ref[i] - delta)).astype(jnp.bfloat16)

    out_t = contract(vall_ref[...], p_ref[...], 0, 0)
    qg_t = contract(kall_ref[...], ds_ref[...], 0, 0) * score_scale
    for j in range(blocks):
        rows = slice(j * BLOCK, (j + 1) * BLOCK)
        base = j * wide
        for result, ref in ((out_t, att_ref), (qg_t, qg_ref)):
            picked = jnp.concatenate(
                [result[:HEAD_DIM, base : base + BLOCK], result[HEAD_DIM:, base + BLOCK : base + wide]], axis=0
            )
            ref[rows, :] = picked.T.astype(jnp.bfloat16)
    for which, (left, right) in enumerate(((ds_ref, qall_ref), (p_ref, gall_ref))):
        grads = contract(left[...], right[...], 1, 0)
        own_ref[which] = grads[BLOCK : BLOCK + own_rows]
        rims_ref[which, :BLOCK] = grads[:BLOCK].astype(jnp.bfloat16)
        rims_ref[which, BLOCK:] = grads[BLOCK + own_rows : near * BLOCK].astype(jnp.bfloat16)
        far_ref[which] = grads[near * BLOCK :].astype(jnp.bfloat16)


def attention(queries, out_grad, key_rows, value_rows, before, after, shared, fetched, bits, chunk):
    tokens_here, width = queries.shape
    blocks = tokens_here // BLOCK
    pairs = width // PAIR // CHUNKS
    start = chunk * pairs
    part_width = width // CHUNKS
    far_rows = (NGLOBAL + NMATCH) * BLOCK
    all_rows = (blocks + 2) * BLOCK + far_rows

    def plain(rows):
        return pl.BlockSpec((rows, PAIR), lambda h: (0, start + h))

    def halves(rows):
        return [pl.BlockSpec((rows, PAIR), lambda h: (0, h)), pl.BlockSpec((rows, PAIR), lambda h: (0, pairs + h))]

    def out(rows, kind):
        return pl.BlockSpec((2, rows, PAIR), lambda h: (0, 0, h)), jax.ShapeDtypeStruct((2, rows, part_width), kind)

    flat = pl.BlockSpec((tokens_here, PAIR), lambda h: (0, h)), jax.ShapeDtypeStruct((tokens_here, part_width), jnp.bfloat16)
    outs = [flat, flat, out(tokens_here, jnp.float32), out(2 * BLOCK, jnp.bfloat16), out(far_rows, jnp.bfloat16)]
    pair_work = HEADS // CHUNKS * tokens_here * SLOTS * BLOCK
    return pl.pallas_call(
        functools.partial(attention_kernel, blocks),
        grid=(pairs,),
        in_specs=[plain(tokens_here)] * 4
        + halves(BLOCK) + halves(BLOCK) + halves(NGLOBAL * BLOCK) + halves(NMATCH * BLOCK)
        + [pl.BlockSpec(bits.shape, lambda h: (0, 0, 0))],
        out_specs=[spec for spec, _ in outs],
        out_shape=[shape for _, shape in outs],
        scratch_shapes=[
            pltpu.VMEM((blocks, SLOTS, BLOCK, BLOCK), jnp.float32),
            pltpu.VMEM((all_rows, PAIR), jnp.bfloat16),
            pltpu.VMEM((all_rows, PAIR), jnp.bfloat16),
            pltpu.VMEM((2 * tokens_here, PAIR), jnp.bfloat16),
            pltpu.VMEM((2 * tokens_here, PAIR), jnp.bfloat16),
            pltpu.VMEM((SLOTS, BLOCK, 2 * BLOCK), jnp.float32),
            pltpu.VMEM((SLOTS, BLOCK, 2 * BLOCK), jnp.float32),
            pltpu.VMEM((all_rows, 2 * tokens_here), jnp.bfloat16),
            pltpu.VMEM((all_rows, 2 * tokens_here), jnp.bfloat16),
        ],
        cost_estimate=pl.CostEstimate(
            flops=pair_work * HEAD_DIM * 2 * 7, bytes_accessed=16 * tokens_here * part_width, transcendentals=pair_work
        ),
        name="block_attention",
    )(queries, out_grad, key_rows, value_rows, before, before, after, after, shared, shared, fetched, fetched, bits)


def partner_of(me, bit):
    flag = (me // 2**bit) % 2
    return flag, me + 2**bit - 2 * 2**bit * flag


def greet(me, cols):
    barrier = pltpu.get_barrier_semaphore()

    def hello(step, carry):
        pl.semaphore_signal(barrier, inc=1, device_id={"col": (me + step) % cols})
        return carry

    lax.fori_loop(1, cols, hello, 0)
    pl.semaphore_wait(barrier, cols - 1)


def bulk_copy(me, cols, turn, from_ref, to_ref, sems):
    step = (turn * (cols // 2 - 1)) % cols
    other = (me + step) % cols
    return pltpu.make_async_remote_copy(
        src_ref=from_ref.at[other],
        dst_ref=to_ref.at[me],
        send_sem=sems[0].at[step],
        recv_sem=sems[1].at[step],
        device_id={"col": other},
    )


def bulk_start(me, cols, lower, upper, from_ref, to_ref, sems):
    def send(step, carry):
        bulk_copy(me, cols, step, from_ref, to_ref, sems).start()
        return carry

    lax.fori_loop(lower, upper, send, 0)


def bulk_wait(me, cols, from_ref, to_ref, sems):
    def finish(step, carry):
        bulk_copy(me, cols, step, from_ref, to_ref, sems).wait()
        return carry

    lax.fori_loop(1, cols, finish, 0)


def groups_of(cols, levels):
    return [1 + (cols - 1) * i // levels for i in range(levels + 1)]


def early_groups(cols, levels):
    return [1] + [cols] * levels


def exchange_kernel(cols, from_ref, to_ref, *sems):
    me = lax.axis_index("col")
    greet(me, cols)
    bulk_start(me, cols, 1, cols, from_ref, to_ref, sems)
    to_ref[me] = from_ref[me]
    bulk_wait(me, cols, from_ref, to_ref, sems)


def direct_exchange(pieces, number):
    cols = pieces.shape[0]
    vmem = pl.BlockSpec(memory_space=pltpu.VMEM)
    return pl.pallas_call(
        functools.partial(exchange_kernel, cols),
        out_shape=jax.ShapeDtypeStruct(pieces.shape, pieces.dtype),
        in_specs=[vmem],
        out_specs=vmem,
        scratch_shapes=[pltpu.SemaphoreType.DMA((cols,))] * 2,
        compiler_params=pltpu.CompilerParams(collective_id=number, has_side_effects=True),
        cost_estimate=pl.CostEstimate(flops=3 * 10**10, bytes_accessed=4 * pieces.size, transcendentals=0),
        name="direct_exchange",
    )(pieces)


def gather_kernel(cols, levels, strip_ref, from_ref, all_ref, to_ref, send_sem, recv_sem, *sems):
    me = lax.axis_index("col")
    greet(me, cols)
    flags = [partner_of(me, levels - 1 - d)[0] for d in range(levels)]
    here = tuple(pl.ds(flag, 1) for flag in flags)
    bounds = groups_of(cols, levels)
    all_ref[here] = strip_ref[...].reshape((1,) * levels + strip_ref.shape)
    for dim in range(levels):
        region = (slice(None),) * dim + here[dim:]
        copy = pltpu.make_async_remote_copy(
            src_ref=all_ref.at[region],
            dst_ref=all_ref.at[region],
            send_sem=send_sem.at[dim],
            recv_sem=recv_sem.at[dim],
            device_id={"col": partner_of(me, levels - 1 - dim)[1]},
        )
        copy.start()
        bulk_start(me, cols, bounds[dim], bounds[dim + 1], from_ref, to_ref, sems)
        if dim == 0:
            to_ref[me] = from_ref[me]
        copy.wait()
    bulk_wait(me, cols, from_ref, to_ref, sems)


def gather_exchange(strip, pieces):
    cols = pieces.shape[0]
    levels = cols.bit_length() - 1
    vmem = pl.BlockSpec(memory_space=pltpu.VMEM)
    out, landed = pl.pallas_call(
        functools.partial(gather_kernel, cols, levels),
        out_shape=[
            jax.ShapeDtypeStruct((2,) * levels + strip.shape, strip.dtype),
            jax.ShapeDtypeStruct(pieces.shape, pieces.dtype),
        ],
        in_specs=[vmem, vmem],
        out_specs=[vmem, vmem],
        scratch_shapes=[pltpu.SemaphoreType.DMA((levels,))] * 2 + [pltpu.SemaphoreType.DMA((cols,))] * 2,
        compiler_params=pltpu.CompilerParams(collective_id=1, has_side_effects=True),
        cost_estimate=pl.CostEstimate(flops=3 * 10**10, bytes_accessed=4 * pieces.size, transcendentals=0),
        name="gather_exchange",
    )(strip, pieces)
    return out.reshape((cols,) + strip.shape), landed


def reduce_kernel(cols, levels, parts_ref, from_ref, sum_ref, to_ref, *scratch):
    landing, sums = scratch[:levels], scratch[levels : 2 * levels - 1]
    send_sem, recv_sem = scratch[2 * levels - 1 : 2 * levels + 1]
    sems = scratch[2 * levels + 1 :]
    me = lax.axis_index("col")
    greet(me, cols)
    bounds = early_groups(cols, levels)
    source = parts_ref
    for bit in range(levels):
        dim = levels - 1 - bit
        flag, partner = partner_of(me, bit)
        lead = (slice(None),) * dim
        tail = (slice(None),) * (bit + 2)
        copy = pltpu.make_async_remote_copy(
            src_ref=source.at[lead + (pl.ds(1 - flag, 1),) + tail],
            dst_ref=landing[bit],
            send_sem=send_sem.at[bit],
            recv_sem=recv_sem.at[bit],
            device_id={"col": partner},
        )
        copy.start()
        bulk_start(me, cols, bounds[bit], bounds[bit + 1], from_ref, to_ref, sems)
        if bit == 0:
            to_ref[me] = from_ref[me]
        copy.wait()
        mine = source[lead + (pl.ds(flag, 1),) + tail]
        total = mine.astype(jnp.float32) + landing[bit][...].astype(jnp.float32)
        if bit < levels - 1:
            source = sums[bit]
            source[...] = total.astype(source.dtype)
        else:
            sum_ref[...] = total.reshape(sum_ref.shape)
    bulk_wait(me, cols, from_ref, to_ref, sems)


def reduce_exchange(parts, pieces):
    cols, rows, width = parts.shape
    levels = cols.bit_length() - 1
    vmem = pl.BlockSpec(memory_space=pltpu.VMEM)
    shapes = [(2,) * (levels - 1 - bit) + (1,) * (bit + 1) + (rows, width) for bit in range(levels)]
    return pl.pallas_call(
        functools.partial(reduce_kernel, cols, levels),
        out_shape=[
            jax.ShapeDtypeStruct((rows, width), jnp.float32),
            jax.ShapeDtypeStruct(pieces.shape, pieces.dtype),
        ],
        in_specs=[vmem, vmem],
        out_specs=[vmem, vmem],
        scratch_shapes=[pltpu.VMEM(shape, parts.dtype if bit < 2 else jnp.float32) for bit, shape in enumerate(shapes)]
        + [pltpu.VMEM(shape, jnp.float32 if bit else parts.dtype) for bit, shape in enumerate(shapes[:-1])]
        + [pltpu.SemaphoreType.DMA((levels,))] * 2 + [pltpu.SemaphoreType.DMA((cols,))] * 2,
        compiler_params=pltpu.CompilerParams(collective_id=2, has_side_effects=True),
        cost_estimate=pl.CostEstimate(flops=3 * 10**10, bytes_accessed=4 * pieces.size, transcendentals=0),
        name="reduce_exchange",
    )(parts.reshape((2,) * levels + (rows, width)), pieces)


def body(queries, key_rows, value_rows, out_grad, dropout_bits, partner, block_pick, global_blocks):
    tokens_here, width = queries.shape
    blocks = tokens_here // BLOCK
    bands, cols = lax.axis_size("row"), lax.axis_size("col")
    band, place = lax.axis_index("row"), lax.axis_index("col")
    rows = BLOCK // cols
    part = width // CHUNKS
    size = bands * cols
    up = [(i, (i + 1) % size) for i in range(size)]
    down = [(j, i) for i, j in up]
    ordering = lax.dynamic_index_in_dim(partner, band, 1, keepdims=False)
    picks = lax.dynamic_index_in_dim(block_pick, band, 1, keepdims=False)
    col_ids = jnp.arange(cols, dtype=jnp.int32)
    hits = ordering[:, :, None] == col_ids[None, None, :]
    inverse = jnp.sum(jnp.where(hits, col_ids[None, :, None], 0), axis=1)
    asked = jnp.sum(jnp.where(hits, picks[:, :, None], 0), axis=1)
    wanted_ids = (ordering * blocks + picks).T.reshape(-1)
    band_start = band * cols * blocks
    global_ids = jnp.clip(global_blocks - band_start, 0, cols * blocks - 1)
    bits = dropout_bits.reshape(blocks, BLOCK, -1).swapaxes(1, 2)
    attended, query_grad, key_grad, value_grad = [], [], [], []
    for chunk in range(CHUNKS):
        lower, upper = chunk * part, (chunk + 1) * part
        both = jnp.concatenate([key_rows[:, lower:upper], value_rows[:, lower:upper]], 1)
        own_strips = both.reshape(blocks, cols, rows, 2 * part).swapaxes(0, 1)
        spread = direct_exchange(own_strips.reshape(cols, blocks * rows, 2 * part), 3)
        strips = spread.reshape(cols * blocks, rows, 2 * part)
        global_strips = jnp.take(strips, global_ids, axis=0)
        owners = global_blocks // (cols * blocks)
        chosen = global_strips
        for step in range(1, bands):
            ring = [(i, (i + step) % bands) for i in range(bands)]
            other = lax.ppermute(global_strips, "row", ring)
            chosen = jnp.where((owners == (band - step) % bands)[:, None, None], other, chosen)
        sent = jnp.take(strips, wanted_ids, axis=0).reshape(cols, NMATCH, rows, 2 * part)
        shared, fetched = gather_exchange(
            chosen.reshape(NGLOBAL * rows, 2 * part), sent.reshape(cols, NMATCH * rows, 2 * part)
        )
        shared = shared.reshape(cols, NGLOBAL, rows, 2 * part).swapaxes(0, 1).reshape(NGLOBAL * BLOCK, 2 * part)
        fetched = fetched.reshape(cols, NMATCH, rows, 2 * part)
        fetched = fetched.swapaxes(0, 1).reshape(NMATCH * BLOCK, 2 * part)
        before = lax.ppermute(both[tokens_here - BLOCK :], ("row", "col"), up)
        after = lax.ppermute(both[:BLOCK], ("row", "col"), down)
        att, qgrad, own, rims, far = attention(
            queries, out_grad, key_rows, value_rows, before, after, shared, fetched, bits, chunk
        )
        attended.append(att)
        query_grad.append(qgrad)
        from_next = lax.ppermute(rims[:, :BLOCK], ("row", "col"), down)
        from_last = lax.ppermute(rims[:, BLOCK:], ("row", "col"), up)
        slots = NGLOBAL + NMATCH
        pieces = far.reshape(2, slots, cols, rows, part).transpose(2, 1, 0, 3, 4)
        strips_sum, landed = reduce_exchange(
            pieces[:, :NGLOBAL].reshape(cols, NGLOBAL * 2 * rows, part),
            pieces[:, NGLOBAL:].reshape(cols, NMATCH * 2 * rows, part),
        )
        landed = landed.reshape(cols, NMATCH, 2, rows, part)
        band_sum = strips_sum.reshape(NGLOBAL, 2, rows, part)
        global_sum = band_sum
        for step in range(1, bands):
            ring = [(i, (i + step) % bands) for i in range(bands)]
            global_sum = global_sum + lax.ppermute(band_sum, "row", ring)
        block_ids = (band_start + jnp.arange(cols * blocks, dtype=jnp.int32)).reshape(cols, blocks)
        local_ids = jnp.arange(blocks, dtype=jnp.int32)
        returned = jnp.zeros((cols, blocks, 2, rows, part), jnp.float32)
        for matching in range(NMATCH):
            moved = jnp.take(landed[:, matching], inverse[matching], axis=0).astype(jnp.float32)
            mine = asked[matching][:, None] == local_ids[None, :]
            returned = returned + jnp.where(mine[:, :, None, None, None], moved[:, None], 0.0)
        for g in range(NGLOBAL):
            mine = block_ids == global_blocks[g]
            returned = returned + jnp.where(mine[:, :, None, None, None], global_sum[g][None, None], 0.0)
        home = direct_exchange(returned.astype(jnp.bfloat16).reshape(cols, blocks * 2 * rows, part), 4)
        home = home.reshape(cols, blocks, 2, rows, part).transpose(2, 1, 0, 3, 4).reshape(2, tokens_here, part)
        total = own + home.astype(jnp.float32)
        room = ((0, 0), (0, tokens_here - BLOCK), (0, 0))
        total = total + jnp.pad(from_last.astype(jnp.float32), room)
        total = total + jnp.pad(from_next.astype(jnp.float32), (room[0], room[1][::-1], room[2]))
        key_grad.append(total[0].astype(jnp.bfloat16))
        value_grad.append(total[1].astype(jnp.bfloat16))
    return tuple(jnp.concatenate(parts, 1) for parts in (attended, query_grad, key_grad, value_grad))


def solution(mesh):
    split = P(("row", "col"), None)
    return jax.shard_map(
        body,
        mesh=mesh,
        in_specs=(split,) * 5 + (P(),) * 3,
        out_specs=(split,) * 4,
        check_vma=False,
    )
```
